512 devices in a mesh: fsdp: 16 (over z), replica: 16 (over x_lo, y, core), tm: 2 (over x_hi).
Axes of the slice: x: 4 (x_hi: 2, x_lo: 2; x = x_hi * 2 + x_lo), y: 4, z: 16, core: 2. Of those that a mesh axis runs over, the one named last changes fastest.
Arguments:
- clip_input: bfloat16 [16, 8, 16, 16, 512], P('replica', 'tm'), may hold values from -6 to 6
- first_kernel: bfloat16 [27, 512, 512], P(None, None, 'fsdp'), may hold values from -0.0546875 to 0.0546875
- second_kernel: bfloat16 [27, 512, 512], P(None, 'fsdp'), may hold values from -0.0546875 to 0.0546875
- out_grad: bfloat16 [16, 2, 4, 4, 512], P('replica', 'tm'), may hold values from -1 to 1
- tap_mix: float32 [2, 27, 27], replicated, may hold values from -0.14 to 1.4
- left_panels: float32 [2, 512, 512], P(None, 'fsdp'), may hold values from -0.05 to 2
- right_panels: float32 [2, 512, 512], P(None, 'fsdp', ('replica', 'tm')), may hold values from -0.05 to 2
Outputs:
- update: bfloat16 [2, 27, 512, 512], P(None, None, 'fsdp', ('replica', 'tm'))
The draws below stay inside these ranges and needn't reach their ends.
All inputs are finite; a program needn't handle non-finite values.
Results may differ from the reference program's by a relative error of at most 0.0049.
Values may be sent and summed in bfloat16 or wider, within the bound.
A program may use at most 128 MiB of HBM per device.

```python
import jax
import jax.numpy as jnp
from jax import lax

CHANNELS = 512
TAPS = 27
FR_DEV = 4
SIDE = 16
CLIPS = 16
FRAMES = 8
N_REPLICA = 16
N_TM = 2


def symmetric_panels(seed_key):
    off_key, diag_key = jax.random.split(seed_key)
    raw_entries = jax.random.uniform(off_key, (2, CHANNELS, CHANNELS), jnp.float32, -0.05, 0.05)
    symmetric = 0.5 * (raw_entries + jnp.swapaxes(raw_entries, 1, 2))
    diag_vals = jax.random.uniform(diag_key, (2, CHANNELS), jnp.float32, 0.5, 2.0)
    identity = jnp.eye(CHANNELS, dtype=jnp.float32)
    return symmetric * (1.0 - identity) + diag_vals[:, :, None] * identity


def draw_left_panels(key, part):
    return symmetric_panels(jax.random.fold_in(key, 11))


def draw_right_panels(key, part):
    return symmetric_panels(jax.random.fold_in(key, 23))


def draw_tap_mix(key, part):
    off_key, diag_key = jax.random.split(jax.random.fold_in(key, 37))
    off_entries = jax.random.uniform(off_key, (2, TAPS, TAPS), jnp.float32, -0.14, 0.14)
    diag_vals = jax.random.uniform(diag_key, (2, TAPS), jnp.float32, 0.6, 1.4)
    identity = jnp.eye(TAPS, dtype=jnp.float32)
    return off_entries * (1.0 - identity) + diag_vals[:, :, None] * identity


def level_of(rng, shape, shards, low, largest):
    loudness, own = 1.0, jax.random.fold_in(rng, 6)
    for axis_at, parts in shards:
        draws = jnp.exp(jax.random.uniform(jax.random.fold_in(own, axis_at), (parts,), jnp.float32, low / len(shards), largest / len(shards)))
        loudness = loudness * jnp.repeat(draws, shape[axis_at] // parts).reshape([-1 if axis == axis_at else 1 for axis in range(len(shape))])
    return loudness


def bell_draw(stream_key, extent, deviation, limit, cuts=(), held_as=jnp.bfloat16):
    entries = deviation * jax.random.normal(stream_key, extent, jnp.float32)
    if cuts:
        entries = entries * level_of(stream_key, extent, cuts, -0.22, 0.18)
    return jnp.clip(entries, -limit, limit).astype(held_as)


def setup_inputs(seed: int = 0) -> dict:
    arg_keys = jax.random.split(jax.random.key(seed), 8)
    clip_input = bell_draw(arg_keys[0], (CLIPS, FRAMES, SIDE, SIDE, CHANNELS), 1.0, 6.0, ((0, 16), (1, 2)))
    first_kernel = bell_draw(arg_keys[1], (TAPS, CHANNELS, CHANNELS), (TAPS * CHANNELS) ** -0.5, 0.0546875, ((2, 16),))
    second_kernel = bell_draw(arg_keys[2], (TAPS, CHANNELS, CHANNELS), (TAPS * CHANNELS) ** -0.5, 0.0546875, ((1, 16),))
    out_grad = bell_draw(arg_keys[3], (CLIPS, FRAMES // 4, SIDE // 4, SIDE // 4, CHANNELS), ((N_REPLICA * N_TM * FR_DEV * SIDE * SIDE // 144) ** -0.5), 1.0, ((0, 16), (1, 2)))
    tap_mix = draw_tap_mix(jax.random.fold_in(arg_keys[7], 71), 0)
    left_panels = draw_left_panels(jax.random.fold_in(arg_keys[7], 71), 0)
    right_panels = draw_right_panels(jax.random.fold_in(arg_keys[7], 71), 0)
    return dict(clip_input=clip_input, first_kernel=first_kernel, second_kernel=second_kernel, out_grad=out_grad, tap_mix=tap_mix, left_panels=left_panels, right_panels=right_panels)


def tap_patches(padded, out_frames, out_side):
    pieces_list = []
    for tap_index in range(TAPS):
        along_time = tap_index // 9
        along_rows = (tap_index // 3) % 3
        along_cols = tap_index % 3
        pieces_list.append(padded[:, along_time:along_time + 2 * out_frames:2, along_rows:along_rows + 2 * out_side:2, along_cols:along_cols + 2 * out_side:2, :])
    return jnp.concatenate(pieces_list, axis=-1)


def spread_back(grad_shape, columns, out_frames, out_side, channels):
    total = jnp.zeros(grad_shape, jnp.float32)
    for tap_index in range(TAPS):
        along_time = tap_index // 9
        along_rows = (tap_index // 3) % 3
        along_cols = tap_index % 3
        total = total.at[:, along_time:along_time + 2 * out_frames:2, along_rows:along_rows + 2 * out_side:2, along_cols:along_cols + 2 * out_side:2, :].add(columns[..., tap_index * channels:(tap_index + 1) * channels])
    return total


def reference(clip_input, first_kernel, second_kernel, out_grad, tap_mix, left_panels, right_panels):
    highest = lax.Precision.HIGHEST
    clip_count = clip_input.shape[0]
    frames = clip_input.shape[1]
    side_cells = clip_input.shape[2]
    channels = clip_input.shape[4]
    half_frames = frames // 2
    half_side = side_cells // 2
    quarter_frames = frames // 4
    quarter_side = side_cells // 4
    padding = ((0, 0), (1, 0), (1, 0), (1, 0), (0, 0))
    padded_input = jnp.pad(clip_input, padding)
    first_patches = tap_patches(padded_input, half_frames, half_side).reshape(-1, TAPS * channels).astype(jnp.float32)
    pre_act = jnp.dot(first_patches, first_kernel.reshape(TAPS * channels, channels).astype(jnp.float32), precision=highest)
    hidden = jax.nn.silu(pre_act).astype(jnp.bfloat16)
    padded_hidden = jnp.pad(hidden.reshape(clip_count, half_frames, half_side, half_side, channels), padding)
    second_patches = tap_patches(padded_hidden, quarter_frames, quarter_side).reshape(-1, TAPS * channels).astype(jnp.float32)
    grad_rows = out_grad.reshape(-1, channels).astype(jnp.float32)
    second_grad = jnp.dot(grad_rows.T, second_patches, precision=highest).reshape(channels, TAPS, channels).transpose(1, 0, 2)
    back_columns = jnp.dot(grad_rows, second_kernel.reshape(TAPS * channels, channels).astype(jnp.float32).T, precision=highest)
    back_columns = back_columns.reshape(clip_count, quarter_frames, quarter_side, quarter_side, TAPS * channels)
    spread = spread_back(padded_hidden.shape, back_columns, quarter_frames, quarter_side, channels)
    hidden_grad = spread[:, 1:, 1:, 1:, :].reshape(-1, channels)
    sigmoid_vals = jax.nn.sigmoid(pre_act)
    pre_grad = (hidden_grad * sigmoid_vals * (1.0 + pre_act * (1.0 - sigmoid_vals))).astype(jnp.bfloat16)
    first_grad = jnp.dot(first_patches.T, pre_grad.astype(jnp.float32), precision=highest).reshape(TAPS, channels, channels)
    stacked = jnp.stack([first_grad, second_grad])
    tap_mixed = jnp.einsum('lst,ltij->lsij', tap_mix, stacked, precision=highest)
    left_done = jnp.einsum('lik,lskj->lsij', left_panels, tap_mixed, precision=highest)
    result = jnp.einsum('lsij,ljk->lsik', left_done, right_panels, precision=highest)
    return result.astype(jnp.bfloat16)
```

```python
import functools

import jax
import jax.numpy as jnp
from jax import lax
from jax.experimental import pallas as pl
from jax.experimental.pallas import tpu as pltpu
from jax.sharding import PartitionSpec as P

TAPS = 27
MESH = pl.DeviceIdType.MESH
F32 = jnp.float32
BF16 = jnp.bfloat16
NZ = 16
NX = 4
NY = 4
COLS = 896


def dot(a, b):
    return lax.dot_general(a, b, (((1,), (0,)), ((), ())), preferred_element_type=F32)


def dot_t(a, b):
    return lax.dot_general(a, b, (((1,), (1,)), ((), ())), preferred_element_type=F32)


def split(v):
    high = v.astype(BF16)
    return high, (v - high.astype(F32)).astype(BF16)


def gather_rows(b, c, rows, wide):
    shape = (64, wide * wide)
    position = lax.broadcasted_iota(jnp.int32, shape, 0)
    cell = lax.broadcasted_iota(jnp.int32, shape, 1)
    yh, xh = position >> 3, position & 7
    if rows == "read":
        hit = cell == (2 * yh + (b - 1)) * wide + 2 * xh + (c - 1)
        if c == 0:
            hit = hit & (xh > 0)
    else:
        yq, xq = cell >> 2, cell & 3
        hit = (yh == 2 * yq + (b - 1)) & (xh == 2 * xq + (c - 1))
    return jnp.where(hit, 1.0, 0.0).astype(BF16)


def kernel(
    x_ref, k1_ref, k2_ref, og_ref, mix_ref, left_ref, right_ref, out_ref,
    patches, spread, og_own, og_in, halo_out, halo_in, lhalo_out, lhalo_in,
    acts, rtiles, rall, xl, mixed32, mixed, mixpad,
    u_send, u_in, u_own, s1_send, s1_in, s2, s2_send, s2_in,
    og_sem, halo_sem, lhalo_sem, act_ssem, act_rsem, rz_ssem, rz_rsem,
    rp_ssem, rp_rsem, rc_sem, uc_ssem, uc_rsem, p1_ssem, p1_rsem, p2_ssem, p2_rsem,
):
    z = lax.axis_index("fsdp")
    rep = lax.axis_index("replica")
    tm = lax.axis_index("tm")
    core = rep % 2
    y = (rep // 2) % NY
    x_lo = rep // (2 * NY)
    xi = tm * 2 + x_lo
    chip = xi * NY + y

    def at(xi_to, y_to, core_to):
        return {"replica": ((xi_to % 2) * NY + y_to) * 2 + core_to, "tm": xi_to // 2}

    def chip_at(d):
        to = (chip + d) % (NX * NY)
        return at(to // NY, to % NY, core)

    def remote(src, dst, ssem, rsem, device):
        return pltpu.make_async_remote_copy(
            src_ref=src, dst_ref=dst, send_sem=ssem, recv_sem=rsem,
            device_id=device, device_id_type=MESH,
        )

    other_core = {"replica": rep + 1 - 2 * core}
    other_half = {"tm": 1 - tm}

    barrier = pltpu.get_barrier_semaphore()

    def greet_z(d, carry):
        pl.semaphore_signal(barrier, inc=1, device_id={"fsdp": (z + d) % NZ}, device_id_type=MESH)
        return carry

    def greet_plane(d, carry):
        pl.semaphore_signal(barrier, inc=1, device_id=chip_at(d), device_id_type=MESH)
        return carry

    lax.fori_loop(1, NZ, greet_z, 0)
    lax.fori_loop(1, NX * NY, greet_plane, 0)
    pl.semaphore_signal(barrier, inc=1, device_id=other_core, device_id_type=MESH)

    select = jnp.concatenate([gather_rows(t // 3, t % 3, "read", 16) for t in range(9)], axis=0)
    for slot, frame in enumerate((0, 2, 1, 3)):
        picked = dot(select, x_ref[frame]).astype(BF16)
        for t in range(9):
            patches[t, slot * 64 : (slot + 1) * 64, :] = picked[t * 64 : (t + 1) * 64]

    lane = lax.broadcasted_iota(jnp.int32, (32, 128), 1)
    first_half = lane < 64
    left0 = split(left_ref[0])
    left1 = split(left_ref[1])
    acc = jnp.zeros((96, 256), F32)
    for t in range(9):
        stack = jnp.concatenate(
            [k1_ref[t], k1_ref[9 + t], k1_ref[18 + t], left0[0], left0[1]], axis=0
        )
        res = dot_t(stack, patches[t])
        acc = acc + res[:96]
        lx = res[96:128] + res[128:160]
        xl[0, 9 + t] = lx[:, :128]
        xl[0, 18 + t] = lx[:, 128:]
        turned = pltpu.roll(lx[:, 128:], 64, 1)
        xl[0, t] = turned
        lhalo_out[t] = turned.astype(BF16)
    turned_pre = pltpu.roll(acc[:32, 128:], 64, 1)
    halo_out[...] = turned_pre

    row = lax.broadcasted_iota(jnp.int32, (32, 128), 0)
    tile = dot(right_ref[0].astype(BF16), jnp.where(lane == row, 1.0, 0.0).astype(BF16))
    tile = tile + dot(right_ref[1].astype(BF16), jnp.where(lane == row + 32, 1.0, 0.0).astype(BF16))
    rtiles[pl.ds(z, 1)] = tile.astype(BF16)[None]

    pl.semaphore_wait(barrier, NZ - 1 + NX * NY - 1 + 1)

    halo = remote(halo_out, halo_in, halo_sem.at[0], halo_sem.at[1], other_half)
    halo.start()
    og_copy = remote(og_ref, og_in, og_sem.at[0], og_sem.at[1], other_half)
    og_copy.start()

    def rz(d, block):
        return remote(
            rtiles.at[z], rtiles.at[block], rz_ssem.at[d - 1], rz_rsem.at[d - 1],
            {"fsdp": (z + d) % NZ},
        )

    def rz_start(d, carry):
        rz(d, z).start()
        return carry

    lax.fori_loop(1, NZ, rz_start, 0)
    lhalo = remote(lhalo_out, lhalo_in, lhalo_sem.at[0], lhalo_sem.at[1], other_half)
    lhalo.start()

    place = jnp.concatenate([gather_rows(t // 3, t % 3, "spread", 4) for t in range(9)], axis=0)
    for r in range(4):
        og_own[0, 4 * r : 4 * r + 4, :] = og_ref[r].astype(F32)
    picked = dot(place, og_own[0].astype(BF16)).astype(BF16)
    for t in range(9):
        spread[t, :64, :] = picked[t * 64 : (t + 1) * 64]
    og_copy.wait_recv()
    keep_next = jnp.where(tm == 0, 1.0, 0.0).astype(F32)
    for r in range(4):
        og_own[1, 4 * r : 4 * r + 4, :] = og_in[r].astype(F32) * keep_next
    picked = dot(place, og_own[1].astype(BF16)).astype(BF16)
    for t in range(9):
        spread[t, 64:, :] = picked[t * 64 : (t + 1) * 64]
    back = jnp.zeros((96, 128), F32)
    for t in range(9):
        stack = jnp.concatenate(
            [k2_ref[t], k2_ref[9 + t], k2_ref[18 + t], left1[0], left1[1]], axis=0
        )
        res = dot_t(stack, spread[t])
        back = back + res[:96]
        lo = res[96:128] + res[128:160]
        xl[1, t] = jnp.where(first_half, 0.0, lo)
        xl[1, 9 + t] = jnp.where(first_half, lo, 0.0)
        xl[1, 18 + t] = jnp.where(first_half, 0.0, pltpu.roll(lo, 64, 1))
    hidden_grad = jnp.where(first_half, back[32:64], pltpu.roll(back[64:96], 64, 1) + back[:32])

    halo.wait_recv()
    keep_prior = jnp.where(tm == 1, 1.0, 0.0).astype(F32)
    pre = acc[32:64, :128] + acc[64:96, 128:]
    pre = pre + jnp.where(first_half, halo_in[...] * keep_prior, turned_pre)
    sig = jax.nn.sigmoid(pre)
    hidden = pre * sig
    pre_grad = hidden_grad * sig * (1.0 + pre * (1.0 - sig))
    acts[pl.ds(z, 1)] = jnp.concatenate([hidden, pre_grad], axis=0).astype(BF16)[None]

    def act(d, block):
        return remote(
            acts.at[z], acts.at[block], act_ssem.at[d - 1], act_rsem.at[d - 1],
            {"fsdp": (z + d) % NZ},
        )

    def act_start(d, carry):
        act(d, z).start()
        return carry

    lax.fori_loop(1, NZ, act_start, 0)

    def rz_wait(d, carry):
        rz(d, (z - d) % NZ).wait_recv()
        return carry

    lax.fori_loop(1, NZ, rz_wait, 0)
    mine = core * NX * NY + chip
    lane16 = lax.broadcasted_iota(jnp.int32, (16, 128), 1) >> 5
    for g in range(4):
        four = [rtiles[4 * g + v].astype(F32) for v in range(4)]
        for layer in range(2):
            piece = jnp.zeros((16, 128), F32)
            for v in range(4):
                shift = (32 * (v - layer)) % 128
                moved = pltpu.roll(four[v], shift, 1) if shift else four[v]
                piece = jnp.where(lane16 == v, moved, piece)
            rall[pl.ds(mine, 1), layer, :, g * 128 : (g + 1) * 128] = piece.astype(BF16)[None]

    def rp(d, block):
        return remote(
            rall.at[mine], rall.at[block], rp_ssem.at[d - 1], rp_rsem.at[d - 1], chip_at(d)
        )

    def rp_start(d, carry):
        rp(d, mine).start()
        return carry

    lax.fori_loop(1, NX * NY, rp_start, 0)

    lhalo.wait_recv()
    for t in range(9):
        xl[0, t] = jnp.where(first_half, lhalo_in[t].astype(F32) * keep_prior, xl[0, t])
    for t in range(27, 32):
        for layer in range(2):
            xl[layer, t] = jnp.zeros((32, 128), F32)
    big_row = lax.broadcasted_iota(jnp.int32, (256, 256), 0)
    big_col = lax.broadcasted_iota(jnp.int32, (256, 256), 1)
    same = (big_row & 7) == (big_col & 7)
    er = lax.broadcasted_iota(jnp.int32, (256, 32), 0)
    ec = lax.broadcasted_iota(jnp.int32, (256, 32), 1)
    expand = jnp.where((er >> 3) == ec, 1.0, 0.0).astype(BF16)
    mixpad[...] = jnp.zeros((2, 32, 32), F32)
    for layer in range(2):
        mixpad[layer, 0:27, 0:27] = mix_ref[layer]
        wide = []
        for part in split(mixpad[layer]):
            tall = dot(expand, part).astype(BF16)
            wide.append(jnp.where(same, dot_t(tall, expand), 0.0).astype(BF16))
        block = jnp.concatenate(
            [xl[layer, :, 8 * q : 8 * q + 8, :].reshape(256, 128) for q in range(4)], axis=1
        )
        high, low = split(block)
        res = dot(wide[0], high) + dot(wide[0], low) + dot(wide[1], high)
        for q in range(4):
            mixed32[:, 8 * q : 8 * q + 8, :] = res[:, 128 * q : 128 * q + 128].reshape(32, 8, 128)
        mixed[layer] = mixed32[0:28].reshape(COLS, 128).astype(BF16)

    def rp_wait(d, carry):
        rp(d, core * NX * NY + (chip - d) % (NX * NY)).wait_recv()
        return carry

    lax.fori_loop(1, NX * NY, rp_wait, 0)
    half = pl.ds(core * NX * NY, NX * NY)
    far_half = pl.ds((1 - core) * NX * NY, NX * NY)
    rc = remote(rall.at[half], rall.at[half], rc_sem.at[0], rc_sem.at[1], other_core)
    rc.start()

    def act_wait(d, carry):
        act(d, (z - d) % NZ).wait_recv()
        return carry

    lax.fori_loop(1, NZ, act_wait, 0)
    own_acts = [acts[:, 32:64, :].reshape(512, 128), acts[:, 0:32, :].reshape(512, 128)]

    def partial(panel_rows, layer):
        turned_act = dot(rall[panel_rows, layer].reshape(256, 512), own_acts[layer])
        high, low = split(turned_act)
        return dot_t(high, mixed[layer]) + dot_t(low, mixed[layer])

    remote(rall.at[far_half], rall.at[far_half], rc_sem.at[0], rc_sem.at[1], other_core).wait_recv()
    uc = []
    for layer in (1, 0):
        res = partial(far_half, layer).astype(BF16)
        for a in range(4):
            for b in range(4):
                spot = (a, b) if layer == 0 else (b, a)
                u_send[(layer, *spot)] = res[(a * 4 + b) * 16 : (a * 4 + b + 1) * 16]
        copy = remote(u_send.at[layer], u_in.at[layer], uc_ssem.at[layer], uc_rsem.at[layer], other_core)
        copy.start()
        uc.append((layer, copy))
    for layer in (1, 0):
        res = partial(half, layer)
        for a in range(4):
            for b in range(4):
                spot = (a, b) if layer == 0 else (b, a)
                u_own[(layer, *spot)] = res[(a * 4 + b) * 16 : (a * 4 + b + 1) * 16]

    first = {0: xi, 1: y}
    second = {0: y, 1: xi}

    def first_to(layer, f):
        return at(f, y, core) if layer == 0 else at(xi, f, core)

    def second_to(layer, f):
        return at(xi, f, core) if layer == 0 else at(f, y, core)

    p1 = {}
    for layer, copy in uc:
        copy.wait_recv()
        for d in range(1, 4):
            f = (first[layer] + d) % 4
            total = u_own[layer, pl.ds(f, 1)] + u_in[layer, pl.ds(f, 1)].astype(F32)
            s1_send[layer, d - 1] = total[0].astype(BF16)
            p1[layer, d] = remote(
                s1_send.at[layer, d - 1], s1_in.at[layer, d - 1],
                p1_ssem.at[layer, d - 1], p1_rsem.at[layer, d - 1], first_to(layer, f),
            )
            p1[layer, d].start()
    p2 = {}
    for layer in (1, 0):
        f = first[layer]
        total = (u_own[layer, pl.ds(f, 1)] + u_in[layer, pl.ds(f, 1)].astype(F32))[0]
        for d in range(1, 4):
            p1[layer, d].wait_recv()
            total = total + s1_in[layer, d - 1].astype(F32)
        s2[layer] = total
        for d in range(1, 4):
            g = (second[layer] + d) % 4
            s2_send[layer, d - 1] = s2[layer, pl.ds(g, 1)][0].astype(BF16)
            p2[layer, d] = remote(
                s2_send.at[layer, d - 1], s2_in.at[layer, d - 1],
                p2_ssem.at[layer, d - 1], p2_rsem.at[layer, d - 1], second_to(layer, g),
            )
            p2[layer, d].start()
    for layer in (1, 0):
        total = s2[layer, pl.ds(second[layer], 1)][0]
        for d in range(1, 4):
            p2[layer, d].wait_recv()
            total = total + s2_in[layer, d - 1].astype(F32)
        for s in range(TAPS):
            out_ref[layer, s] = total[:, 32 * s : 32 * s + 32].astype(BF16)

    halo.wait_send()
    og_copy.wait_send()
    lhalo.wait_send()
    rc.wait_send()

    def z_sent(d, carry):
        rz(d, z).wait_send()
        act(d, z).wait_send()
        rp(d, mine).wait_send()
        return carry

    lax.fori_loop(1, NZ, z_sent, 0)
    for layer, copy in uc:
        copy.wait_send()
        for d in range(1, 4):
            p1[layer, d].wait_send()
            p2[layer, d].wait_send()


def shards(clip_input, first_kernel, second_kernel, out_grad, tap_mix, left_panels, right_panels):
    vmem = functools.partial(pltpu.VMEM)
    dma = pltpu.SemaphoreType.DMA
    operands = (
        clip_input.reshape(4, 256, 512),
        first_kernel.swapaxes(1, 2),
        second_kernel,
        out_grad.reshape(4, 4, 512),
        tap_mix,
        left_panels,
        right_panels.swapaxes(1, 2),
    )
    spec = pl.BlockSpec(memory_space=pltpu.VMEM)
    out = pl.pallas_call(
        kernel,
        name="shampoo_update",
        out_shape=jax.ShapeDtypeStruct((2, TAPS, 16, 32), BF16),
        in_specs=[spec] * len(operands),
        out_specs=spec,
        scratch_shapes=[
            vmem((9, 256, 512), BF16),
            vmem((9, 128, 512), BF16),
            vmem((2, 16, 512), F32),
            vmem((4, 4, 512), BF16),
            vmem((32, 128), F32),
            vmem((32, 128), F32),
            vmem((9, 32, 128), BF16),
            vmem((9, 32, 128), BF16),
            vmem((NZ, 64, 128), BF16),
            vmem((NZ, 16, 128), BF16),
            vmem((2 * NX * NY, 2, 16, 512), BF16),
            vmem((2, 32, 32, 128), F32),
            vmem((32, 32, 128), F32),
            vmem((2, COLS, 128), BF16),
            vmem((2, 32, 32), F32),
            vmem((2, 4, 4, 16, COLS), BF16),
            vmem((2, 4, 4, 16, COLS), BF16),
            vmem((2, 4, 4, 16, COLS), F32),
            vmem((2, 3, 4, 16, COLS), BF16),
            vmem((2, 3, 4, 16, COLS), BF16),
            vmem((2, 4, 16, COLS), F32),
            vmem((2, 3, 16, COLS), BF16),
            vmem((2, 3, 16, COLS), BF16),
            dma((2,)), dma((2,)), dma((2,)),
            dma((NZ - 1,)), dma((NZ - 1,)), dma((NZ - 1,)), dma((NZ - 1,)),
            dma((NX * NY - 1,)), dma((NX * NY - 1,)),
            dma((2,)), dma((2,)), dma((2,)),
            dma((2, 3)), dma((2, 3)), dma((2, 3)), dma((2, 3)),
        ],
        compiler_params=pltpu.CompilerParams(collective_id=0, has_side_effects=True),
    )(*operands)
    return out.swapaxes(2, 3)


def solution(mesh):
    in_specs = (
        P("replica", "tm", None, None, None),
        P(None, None, "fsdp"),
        P(None, "fsdp", None),
        P("replica", "tm", None, None, None),
        P(),
        P(None, "fsdp", None),
        P(None, "fsdp", ("replica", "tm")),
    )
    out_specs = P(None, None, "fsdp", ("replica", "tm"))
    return jax.shard_map(shards, mesh=mesh, in_specs=in_specs, out_specs=out_specs, check_vma=False)
```

```python
import jax
import jax.numpy as jnp
from jax import lax
from jax.experimental import pallas as pl
from jax.experimental.pallas import tpu as pltpu
from jax.sharding import PartitionSpec as P

TAPS = 27
MESH = pl.DeviceIdType.MESH
F32 = jnp.float32
BF16 = jnp.bfloat16
NZ = 16
NX = 4
NY = 4
COLS = 896


def dot(a, b):
    return lax.dot_general(a, b, (((1,), (0,)), ((), ())), preferred_element_type=F32)


def dot_t(a, b):
    return lax.dot_general(a, b, (((1,), (1,)), ((), ())), preferred_element_type=F32)


def split(v):
    high = v.astype(BF16)
    return high, (v - high.astype(F32)).astype(BF16)


def gather_rows(b, c, rows, wide):
    shape = (64, wide * wide)
    position = lax.broadcasted_iota(jnp.int32, shape, 0)
    cell = lax.broadcasted_iota(jnp.int32, shape, 1)
    yh, xh = position >> 3, position & 7
    if rows == "read":
        hit = cell == (2 * yh + (b - 1)) * wide + 2 * xh + (c - 1)
        if c == 0:
            hit = hit & (xh > 0)
    else:
        yq, xq = cell >> 2, cell & 3
        hit = (yh == 2 * yq + (b - 1)) & (xh == 2 * xq + (c - 1))
    return jnp.where(hit, 1.0, 0.0).astype(BF16)


def kernel(
    x_hbm, k1_hbm, k2_hbm, og_hbm, mix_hbm, left_hbm, right_hbm, out_ref,
    x_ref, k1_ref, k2_ref, og_ref, mix_ref, left_ref, right_ref,
    patches, spread, og_wide, halo_out, halo_in, lhalo_out, lhalo_in,
    acts, acts_far, rtiles, rall, xl, mixed32, mixed, mixed_far, mixpad,
    u, p1_send, p1_in, s2, s2_send, s2_in,
    in_sem, halo_sem, lhalo_sem, act_ssem, act_rsem, rz_ssem, rz_rsem,
    rp_ssem, rp_rsem, cf_ssem, cf_rsem, mc_ssem, mc_rsem, p1_ssem, p1_rsem, p2_ssem, p2_rsem,
):
    z = lax.axis_index("fsdp")
    rep = lax.axis_index("replica")
    tm = lax.axis_index("tm")
    core = rep % 2
    y = (rep // 2) % NY
    x_lo = rep // (2 * NY)
    xi = tm * 2 + x_lo
    chip = xi * NY + y

    def at(xi_to, y_to):
        return {"replica": ((xi_to % 2) * NY + y_to) * 2 + core, "tm": xi_to // 2}

    def chip_at(d):
        to = (chip + d) % (NX * NY)
        return at(to // NY, to % NY)

    def remote(src, dst, ssem, rsem, device):
        return pltpu.make_async_remote_copy(
            src_ref=src, dst_ref=dst, send_sem=ssem, recv_sem=rsem,
            device_id=device, device_id_type=MESH,
        )

    other_core = {"replica": rep + 1 - 2 * core}
    other_half = {"tm": 1 - tm}

    fetch = [
        pltpu.make_async_copy(src, dst, in_sem.at[n])
        for n, (src, dst) in enumerate(
            [(x_hbm.at[f], x_ref.at[f]) for f in range(4)]
            + [
                (right_hbm, right_ref), (left_hbm, left_ref), (k1_hbm, k1_ref),
                (og_hbm, og_ref), (k2_hbm, k2_ref), (mix_hbm, mix_ref),
            ]
        )
    ]
    for copy in fetch:
        copy.start()

    barrier = pltpu.get_barrier_semaphore()

    def greet(device):
        pl.semaphore_signal(barrier, inc=1, device_id=device, device_id_type=MESH)

    for d in (4, 12, 3, 13, 2, 14, 1, 15):
        greet({"fsdp": (z + d) % NZ})

    def greet_plane(d, carry):
        greet(chip_at(d))
        return carry

    lax.fori_loop(1, NX * NY, greet_plane, 0)
    greet(other_core)

    lane = lax.broadcasted_iota(jnp.int32, (32, 128), 1)
    first_half = lane < 64
    is_first = jnp.where(tm == 0, 1.0, 0.0).astype(F32)
    is_last = 1.0 - is_first

    fetch[4].wait()
    row = lax.broadcasted_iota(jnp.int32, (32, 128), 0)
    tile = dot(right_ref[0].astype(BF16), jnp.where(lane == row, 1.0, 0.0).astype(BF16))
    tile = tile + dot(right_ref[1].astype(BF16), jnp.where(lane == row + 32, 1.0, 0.0).astype(BF16))
    rtiles[pl.ds(z, 1)] = tile.astype(BF16)[None]

    select = jnp.concatenate([gather_rows(t // 3, t % 3, "read", 16) for t in range(9)], axis=0)
    for slot, frame in enumerate((0, 2, 1, 3)):
        fetch[frame].wait()
        picked = dot(select, x_ref[frame]).astype(BF16)
        for t in range(9):
            patches[t, slot * 64 : (slot + 1) * 64, :] = picked[t * 64 : (t + 1) * 64]

    fetch[5].wait()
    left0 = split(left_ref[0])
    left1 = split(left_ref[1])
    fetch[6].wait()
    acc = jnp.zeros((96, 256), F32)
    for t in range(9):
        stack = jnp.concatenate(
            [k1_ref[t], k1_ref[9 + t], k1_ref[18 + t], left0[0], left0[1]], axis=0
        )
        res = dot_t(stack, patches[t])
        acc = acc + res[:96]
        lx = res[96:128] + res[128:160]
        xl[0, 9 + t] = lx[:, :128]
        xl[0, 18 + t] = lx[:, 128:]
        xl[0, t] = pltpu.roll(lx[:, 128:], 64, 1)
    turned_pre = pltpu.roll(acc[:32, 128:], 64, 1)

    pl.semaphore_wait(barrier, 8 + NX * NY - 1 + 1)

    class Ring:
        def __init__(self, buf, ssem, rsem):
            self.buf, self.ssem, self.rsem = buf, ssem, rsem

        def copy(self, block, d, device):
            return remote(
                self.buf.at[block], self.buf.at[block],
                self.ssem.at[d - 1], self.rsem.at[d - 1], {"fsdp": device},
            )

        def start(self):
            for e in (4, 3, 2, 1):
                self.copy(z, e, (z + e) % NZ).start()
                self.copy(z, NZ - e, (z + NZ - e) % NZ).start()

        def wait(self, d):
            self.copy((z + NZ - d) % NZ, d, (z + d) % NZ).wait_recv()

        def forward(self):
            self.wait(4)
            for k in (4, 3, 2, 1):
                self.copy((z + NZ - 4) % NZ, 4 + k, (z + k) % NZ).start()
            self.wait(12)
            for k in (3, 2, 1):
                self.copy((z + 4) % NZ, 12 - k, (z + NZ - k) % NZ).start()

        def sent(self):
            for d in range(1, NZ):
                self.copy(z, d, (z + d) % NZ).wait_send()

    rz = Ring(rtiles, rz_ssem, rz_rsem)
    act = Ring(acts, act_ssem, act_rsem)
    rz.start()

    place = jnp.concatenate([gather_rows(t // 3, t % 3, "spread", 4) for t in range(9)], axis=0)
    fetch[7].wait()
    for r in range(4):
        og_wide[4 * r : 4 * r + 4, :] = og_ref[r].astype(F32)
    picked = dot(place, og_wide[...].astype(BF16)).astype(BF16)
    for t in range(9):
        spread[t, :64, :] = picked[t * 64 : (t + 1) * 64]
        spread[t, 64:, :] = picked[t * 64 : (t + 1) * 64]
    fetch[8].wait()
    back = jnp.zeros((96, 128), F32)
    for t in range(9):
        stack = jnp.concatenate(
            [k2_ref[t], k2_ref[9 + t], k2_ref[18 + t], left1[0], left1[1]], axis=0
        )
        res = dot_t(stack, spread[t])
        back = back + res[:96]
        lo = res[96:128] + res[128:160]
        xl[1, 9 + t] = jnp.where(first_half, lo, 0.0)
        xl[1, 18 + t] = jnp.where(first_half, 0.0, lo)
        lhalo_out[t] = (xl[0, t] * is_first + lo * is_last).astype(BF16)
    halo_out[...] = turned_pre * is_first + back[:32] * is_last
    halo = remote(halo_out, halo_in, halo_sem.at[0], halo_sem.at[1], other_half)
    halo.start()

    fetch[9].wait()
    big_row = lax.broadcasted_iota(jnp.int32, (256, 256), 0)
    big_col = lax.broadcasted_iota(jnp.int32, (256, 256), 1)
    same = (big_row & 7) == (big_col & 7)
    er = lax.broadcasted_iota(jnp.int32, (256, 32), 0)
    ec = lax.broadcasted_iota(jnp.int32, (256, 32), 1)
    expand = jnp.where((er >> 3) == ec, 1.0, 0.0).astype(BF16)
    mixpad[...] = jnp.zeros((2, 32, 32), F32)
    wide = []
    for layer in range(2):
        mixpad[layer, 0:27, 0:27] = mix_ref[:, layer, :]
        for part in split(mixpad[layer]):
            tall = dot(expand, part).astype(BF16)
            wide.append(jnp.where(same, dot_t(tall, expand), 0.0).astype(BF16))

    halo.wait_recv()
    received = halo_in[...]
    pre = acc[32:64, :128] + acc[64:96, 128:]
    pre = pre + jnp.where(first_half, received * is_last, turned_pre)
    hidden_grad = jnp.where(first_half, back[32:64], back[64:96] + received * is_first)
    sig = jax.nn.sigmoid(pre)
    hidden = pre * sig
    pre_grad = hidden_grad * sig * (1.0 + pre * (1.0 - sig))
    acts[pl.ds(z, 1)] = jnp.concatenate([hidden, pre_grad], axis=0).astype(BF16)[None]
    act.start()

    def share(d):
        block = (z + NZ - d) % NZ
        return remote(acts.at[block], acts_far.at[block], cf_ssem.at[d], cf_rsem.at[d], other_core)

    share(0).start()
    lhalo = remote(lhalo_out, lhalo_in, lhalo_sem.at[0], lhalo_sem.at[1], other_half)
    lhalo.start()

    rz.forward()
    act.forward()

    for d in (1, 15, 2, 14, 3, 13, 5, 11, 6, 10, 7, 9, 8):
        rz.wait(d)
    lane16 = lax.broadcasted_iota(jnp.int32, (16, 128), 1) >> 5
    for g in range(4):
        four = [rtiles[4 * g + v].astype(F32) for v in range(4)]
        for layer in range(2):
            piece = jnp.zeros((16, 128), F32)
            for v in range(4):
                shift = (32 * (v - layer)) % 128
                moved = pltpu.roll(four[v], shift, 1) if shift else four[v]
                piece = jnp.where(lane16 == v, moved, piece)
            rall[layer, pl.ds(chip, 1), :, g * 128 : (g + 1) * 128] = piece.astype(BF16)[None]

    def rp(layer, d, block):
        return remote(
            rall.at[layer, block], rall.at[layer, block],
            rp_ssem.at[layer, d - 1], rp_rsem.at[layer, d - 1], chip_at(d),
        )

    for layer in (1, 0):

        def rp_start(d, carry, layer=layer):
            rp(layer, d, chip).start()
            return carry

        lax.fori_loop(1, NX * NY, rp_start, 0)

    lhalo.wait_recv()
    for t in range(9):
        got = lhalo_in[t].astype(F32)
        xl[0, t] = jnp.where(first_half, got * is_last, xl[0, t])
        xl[1, t] = jnp.where(first_half, 0.0, got * is_first)
    mc = {}
    for layer in (1, 0):
        for t in range(27, 32):
            xl[layer, t] = jnp.zeros((32, 128), F32)
        block = jnp.concatenate(
            [xl[layer, :, 8 * q : 8 * q + 8, :].reshape(256, 128) for q in range(4)], axis=1
        )
        high, low = split(block)
        res = dot(wide[2 * layer], high) + dot(wide[2 * layer], low) + dot(wide[2 * layer + 1], high)
        for q in range(4):
            mixed32[:, 8 * q : 8 * q + 8, :] = res[:, 128 * q : 128 * q + 128].reshape(32, 8, 128)
        mixed[layer] = mixed32[0:28].reshape(COLS, 128).astype(BF16)
        mc[layer] = remote(
            mixed.at[layer], mixed_far.at[layer], mc_ssem.at[layer], mc_rsem.at[layer], other_core
        )
        mc[layer].start()

    for d in (4, 12):
        share(d).start()
    for d in (1, 15, 2, 14, 3, 13, 5, 11, 6, 10, 7, 9, 8):
        act.wait(d)
        share(d).start()
    for d in range(NZ):
        share(d).wait_recv()

    first = {0: xi, 1: y}
    second = {0: y, 1: xi}

    def first_to(layer, f):
        return at(f, y) if layer == 0 else at(xi, f)

    def second_to(layer, f):
        return at(xi, f) if layer == 0 else at(f, y)

    lower, upper = pl.ds(0, 2), pl.ds(2, 2)

    def send1(layer, n, step):
        return remote(
            p1_send.at[layer, n], p1_in.at[layer, n], p1_ssem.at[layer, n], p1_rsem.at[layer, n],
            first_to(layer, (first[layer] + step) % 4),
        )

    for layer in (1, 0):

        def rp_wait(d, carry, layer=layer):
            rp(layer, d, (chip + NX * NY - d) % (NX * NY)).wait_recv()
            return carry

        lax.fori_loop(1, NX * NY, rp_wait, 0)
        mc[layer].wait_recv()
        rows = pl.ds(0, 32) if layer == 1 else pl.ds(32, 32)
        both = jnp.concatenate(
            [acts[:, rows, :].reshape(512, 128), acts_far[:, rows, :].reshape(512, 128)], axis=1
        )
        turned_act = dot(rall[layer].reshape(256, 512), both)
        high, low = split(turned_act)
        mix = jnp.concatenate([mixed[layer], mixed_far[layer]], axis=1)
        res = dot_t(high, mix) + dot_t(low, mix)
        for a in range(4):
            for b in range(4):
                spot = (a, b) if layer == 0 else (b, a)
                u[(layer, *spot)] = res[(a * 4 + b) * 16 : (a * 4 + b + 1) * 16]
        f = first[layer]
        for n, off, part, step in (
            (0, 2, lower, 1), (1, 2, upper, 3), (2, 1, upper, 1), (3, 3, lower, 3),
        ):
            p1_send[layer, n] = u[layer, pl.ds((f + off) % 4, 1), part][0].astype(BF16)
            send1(layer, n, step).start()

    for layer in (1, 0):
        f = first[layer]
        for n, source, off, part, step in ((4, 0, 1, lower, 1), (5, 1, 3, upper, 3)):
            send1(layer, source, step).wait_recv()
            total = u[layer, pl.ds((f + off) % 4, 1), part][0] + p1_in[layer, source].astype(F32)
            p1_send[layer, n] = total.astype(BF16)
            send1(layer, n, step).start()
    p2 = {}
    for layer in (1, 0):
        f = first[layer]
        for direct, passed, part in ((3, 4, lower), (2, 5, upper)):
            send1(layer, direct, 1).wait_recv()
            send1(layer, passed, 1).wait_recv()
            total = u[layer, pl.ds(f, 1), part][0]
            total = total + p1_in[layer, direct].astype(F32) + p1_in[layer, passed].astype(F32)
            s2[layer, part] = total
        for d in range(1, 4):
            g = (second[layer] + d) % 4
            s2_send[layer, d - 1] = s2[layer, pl.ds(g, 1)][0].astype(BF16)
            p2[layer, d] = remote(
                s2_send.at[layer, d - 1], s2_in.at[layer, d - 1],
                p2_ssem.at[layer, d - 1], p2_rsem.at[layer, d - 1], second_to(layer, g),
            )
            p2[layer, d].start()
    for layer in (1, 0):
        total = s2[layer, pl.ds(second[layer], 1)][0]
        for d in range(1, 4):
            p2[layer, d].wait_recv()
            total = total + s2_in[layer, d - 1].astype(F32)
        for s in range(TAPS):
            out_ref[layer, s] = total[:, 32 * s : 32 * s + 32].astype(BF16)

    halo.wait_send()
    lhalo.wait_send()
    rz.sent()
    act.sent()
    for d in range(NZ):
        share(d).wait_send()
    for layer in (1, 0):

        def rp_sent(d, carry, layer=layer):
            rp(layer, d, chip).wait_send()
            return carry

        lax.fori_loop(1, NX * NY, rp_sent, 0)
        mc[layer].wait_send()
        for n in range(6):
            send1(layer, n, 1).wait_send()
        for d in range(1, 4):
            p2[layer, d].wait_send()


def shards(clip_input, first_kernel, second_kernel, out_grad, tap_mix, left_panels, right_panels):
    vmem = pltpu.VMEM
    dma = pltpu.SemaphoreType.DMA
    operands = (
        clip_input.reshape(4, 256, 512),
        first_kernel.swapaxes(1, 2),
        second_kernel,
        out_grad.reshape(4, 4, 512),
        tap_mix.swapaxes(0, 1),
        left_panels,
        right_panels.swapaxes(1, 2),
    )
    out = pl.pallas_call(
        kernel,
        name="shampoo_update",
        out_shape=jax.ShapeDtypeStruct((2, TAPS, 16, 32), BF16),
        in_specs=[pl.BlockSpec(memory_space=pl.ANY)] * len(operands),
        out_specs=pl.BlockSpec(memory_space=pltpu.VMEM),
        scratch_shapes=[
            *(vmem(v.shape, v.dtype) for v in operands),
            vmem((9, 256, 512), BF16),
            vmem((9, 128, 512), BF16),
            vmem((16, 512), F32),
            vmem((32, 128), F32),
            vmem((32, 128), F32),
            vmem((9, 32, 128), BF16),
            vmem((9, 32, 128), BF16),
            vmem((NZ, 64, 128), BF16),
            vmem((NZ, 64, 128), BF16),
            vmem((NZ, 16, 128), BF16),
            vmem((2, NX * NY, 16, 512), BF16),
            vmem((2, 32, 32, 128), F32),
            vmem((32, 32, 128), F32),
            vmem((2, COLS, 128), BF16),
            vmem((2, COLS, 128), BF16),
            vmem((2, 32, 32), F32),
            vmem((2, 4, 4, 16, COLS), F32),
            vmem((2, 6, 2, 16, COLS), BF16),
            vmem((2, 6, 2, 16, COLS), BF16),
            vmem((2, 4, 16, COLS), F32),
            vmem((2, 3, 16, COLS), BF16),
            vmem((2, 3, 16, COLS), BF16),
            dma((10,)), dma((2,)), dma((2,)),
            dma((NZ - 1,)), dma((NZ - 1,)), dma((NZ - 1,)), dma((NZ - 1,)),
            dma((2, NX * NY - 1)), dma((2, NX * NY - 1)),
            dma((NZ,)), dma((NZ,)), dma((2,)), dma((2,)),
            dma((2, 6)), dma((2, 6)), dma((2, 3)), dma((2, 3)),
        ],
        compiler_params=pltpu.CompilerParams(collective_id=0, has_side_effects=True),
    )(*operands)
    return out.swapaxes(2, 3)


def solution(mesh):
    in_specs = (
        P("replica", "tm", None, None, None),
        P(None, None, "fsdp"),
        P(None, "fsdp", None),
        P("replica", "tm", None, None, None),
        P(),
        P(None, "fsdp", None),
        P(None, "fsdp", ("replica", "tm")),
    )
    out_specs = P(None, None, "fsdp", ("replica", "tm"))
    return jax.shard_map(shards, mesh=mesh, in_specs=in_specs, out_specs=out_specs, check_vma=False)
```

```python
import jax
import jax.numpy as jnp
from jax import lax
from jax.experimental import pallas as pl
from jax.experimental.pallas import tpu as pltpu
from jax.sharding import PartitionSpec as P

TAPS = 27
MESH = pl.DeviceIdType.MESH
F32 = jnp.float32
BF16 = jnp.bfloat16
NZ = 16
NX = 4
NY = 4
COLS = 896


def rem(a, n):
    return lax.rem(a, jnp.int32(n))


def div(a, n):
    return lax.div(a, jnp.int32(n))


def dot(a, b):
    return lax.dot_general(a, b, (((1,), (0,)), ((), ())), preferred_element_type=F32)


def dot_t(a, b):
    return lax.dot_general(a, b, (((1,), (1,)), ((), ())), preferred_element_type=F32)


def split(v):
    high = v.astype(BF16)
    return high, (v - high.astype(F32)).astype(BF16)


def gather_rows(b, c, rows, wide):
    shape = (64, wide * wide)
    position = lax.broadcasted_iota(jnp.int32, shape, 0)
    cell = lax.broadcasted_iota(jnp.int32, shape, 1)
    yh, xh = position >> 3, position & 7
    if rows == "read":
        hit = cell == (2 * yh + (b - 1)) * wide + 2 * xh + (c - 1)
        if c == 0:
            hit = hit & (xh > 0)
    else:
        yq, xq = cell >> 2, cell & 3
        hit = (yh == 2 * yq + (b - 1)) & (xh == 2 * xq + (c - 1))
    return jnp.where(hit, 1.0, 0.0).astype(BF16)


def kernel(
    x_hbm, k1_hbm, k2_hbm, og_hbm, mix_hbm, left_hbm, right_hbm, out_ref,
    x_ref, k1_ref, k2_ref, og_ref, mix_ref, left_ref, right_ref,
    patches, spread, og_wide, halo_out, halo_in, lhalo_out, lhalo_in,
    acts, acts_far, rtiles, rall, xl, mixed32, mixed, mixed_far, mixpad,
    u, p1_send, p1_in, s2_send, s2_in,
    in_sem, halo_sem, lhalo_sem, act_ssem, act_rsem, rz_ssem, rz_rsem,
    rp_sem, cf_sem, mc_sem, p1_ssem, p1_rsem, p2_sem,
):
    z = lax.axis_index("fsdp")
    rep = lax.axis_index("replica")
    tm = lax.axis_index("tm")
    core = rem(rep, 2)
    y = rem(div(rep, 2), NY)
    x_lo = div(rep, 2 * NY)
    xi = tm * 2 + x_lo
    chip = xi * NY + y

    x_at = [rem(xi + d, NX) for d in range(NX)]
    x_part = [(rem(v, 2) * 2 * NY, div(v, 2)) for v in x_at]
    y_part = [rem(y + d, NY) * 2 + core for d in range(NY)]
    plane = [(dx, dy) for dx in (2, 1, 3, 0) for dy in (2, 1, 3, 0) if dx or dy]

    def at(dx, dy):
        return {"replica": x_part[dx][0] + y_part[dy], "tm": x_part[dx][1]}

    def up(d):
        return rem(z + d, NZ)

    def remote(src, dst, ssem, rsem, device):
        return pltpu.make_async_remote_copy(
            src_ref=src, dst_ref=dst, send_sem=ssem, recv_sem=rsem,
            device_id=device, device_id_type=MESH,
        )

    other_core = {"replica": rep + 1 - 2 * core}
    other_half = {"tm": 1 - tm}

    fetch = [
        pltpu.make_async_copy(src, dst, in_sem.at[n])
        for n, (src, dst) in enumerate(
            [(x_hbm.at[f], x_ref.at[f]) for f in range(4)]
            + [
                (right_hbm, right_ref), (left_hbm, left_ref), (k1_hbm, k1_ref),
                (og_hbm, og_ref), (k2_hbm, k2_ref), (mix_hbm, mix_ref),
            ]
        )
    ]
    for n in (1, 3, 6, 7, 8, 4, 0, 2, 5, 9):
        fetch[n].start()

    barrier = pltpu.get_barrier_semaphore()

    def greet(device):
        pl.semaphore_signal(barrier, inc=1, device_id=device, device_id_type=MESH)

    for d in (4, 12, 3, 13, 2, 14, 1, 15):
        greet({"fsdp": up(d)})

    for dx, dy in plane:
        greet(at(dx, dy))
    greet(other_core)

    lane = lax.broadcasted_iota(jnp.int32, (32, 128), 1)
    first_half = lane < 64
    is_first = jnp.where(tm == 0, 1.0, 0.0).astype(F32)
    is_last = 1.0 - is_first

    select = jnp.concatenate([gather_rows(t // 3, t % 3, "read", 16) for t in range(9)], axis=0)

    def pick(pair, frames):
        for slot, frame in enumerate(frames):
            fetch[frame].wait()
            picked = dot(select, x_ref[frame]).astype(BF16)
            for t in range(9):
                patches[pair, t, slot * 64 : (slot + 1) * 64, :] = picked[t * 64 : (t + 1) * 64]

    pick(1, (1, 3))
    fetch[6].wait()
    odd = jnp.zeros((64, 128), F32)
    for t in range(9):
        odd = odd + dot_t(jnp.concatenate([k1_ref[t], k1_ref[18 + t]], axis=0), patches[1, t])
    turned_pre = pltpu.roll(odd[:32], 64, 1)

    fetch[4].wait()
    row = lax.broadcasted_iota(jnp.int32, (32, 128), 0)
    tile = dot(right_ref[0].astype(BF16), jnp.where(lane == row, 1.0, 0.0).astype(BF16))
    tile = tile + dot(right_ref[1].astype(BF16), jnp.where(lane == row + 32, 1.0, 0.0).astype(BF16))
    rtiles[pl.ds(z, 1)] = tile.astype(BF16)[None]

    class Ring:
        def __init__(self, buf, ssem, rsem, group):
            self.buf, self.ssem, self.rsem, self.group = buf, ssem, rsem, group

        def copy(self, back, d):
            block = up(NZ - back)
            gap = (back + d) % NZ
            kind = {4: 0, 12: 1}.get(gap)
            kind = self.group(block, gap) if kind is None else kind
            return remote(
                self.buf.at[block], self.buf.at[block], self.ssem.at[0], self.rsem.at[kind],
                {"fsdp": up(d)},
            )

        def start(self):
            for e in (4, 3, 2, 1):
                self.copy(0, e).start()
                self.copy(0, NZ - e).start()

        def arrived(self, count, kind):
            part = self.buf.at[pl.ds(0, count)]
            remote(part, part, self.ssem.at[0], self.rsem.at[kind], {"fsdp": up(1)}).wait_recv()

        def forward(self):
            self.arrived(1, 0)
            for k in (4, 3, 2, 1):
                self.copy(4, k).start()
            self.arrived(1, 1)
            for k in (3, 2, 1):
                self.copy(12, NZ - k).start()

        def sent(self):
            part = self.buf.at[pl.ds(0, NZ - 1)]
            remote(part, part, self.ssem.at[0], self.rsem.at[0], {"fsdp": up(1)}).wait_send()

    rz = Ring(rtiles, rz_ssem, rz_rsem, lambda block, gap: 2 + div(block, 4))
    act = Ring(acts, act_ssem, act_rsem, lambda block, gap: gap - 2 if 4 < gap < 12 else 2)
    place = jnp.concatenate([gather_rows(t // 3, t % 3, "spread", 4) for t in range(9)], axis=0)
    fetch[7].wait()
    for r in range(4):
        og_wide[4 * r : 4 * r + 4, :] = og_ref[r].astype(F32)
    picked = dot(place, og_wide[...].astype(BF16)).astype(BF16)
    for t in range(9):
        spread[t, :64, :] = picked[t * 64 : (t + 1) * 64]
        spread[t, 64:, :] = picked[t * 64 : (t + 1) * 64]
    fetch[8].wait()
    back = jnp.zeros((96, 128), F32)
    for t in range(9):
        stack = jnp.concatenate([k2_ref[t], k2_ref[9 + t], k2_ref[18 + t]], axis=0)
        back = back + dot_t(stack, spread[t])
    halo_out[...] = turned_pre * is_first + back[:32] * is_last

    pl.semaphore_wait(barrier, 8 + NX * NY - 1 + 1)

    halo = remote(halo_out, halo_in, halo_sem.at[0], halo_sem.at[1], other_half)
    halo.start()
    rz.start()

    pick(0, (0, 2))
    even = jnp.zeros((32, 128), F32)
    for t in range(9):
        even = even + dot_t(k1_ref[9 + t], patches[0, t])

    rz.forward()

    halo.wait_recv()
    received = halo_in[...]
    pre = even + odd[32:] + jnp.where(first_half, received * is_last, turned_pre)
    hidden_grad = jnp.where(first_half, back[32:64], back[64:96] + received * is_first)
    sig = jax.nn.sigmoid(pre)
    hidden = pre * sig
    pre_grad = hidden_grad * sig * (1.0 + pre * (1.0 - sig))
    acts[pl.ds(z, 1)] = jnp.concatenate([hidden, pre_grad], axis=0).astype(BF16)[None]
    act.start()

    def share(d):
        block = up(NZ - d)
        return remote(acts.at[block], acts_far.at[block], cf_sem.at[0], cf_sem.at[1], other_core)

    share(0).start()

    fetch[5].wait()
    left0 = jnp.concatenate(split(left_ref[0]), axis=0)
    left1 = jnp.concatenate(split(left_ref[1]), axis=0)
    for t in range(9):
        res = dot_t(left0, patches[1, t])
        lx = res[:32] + res[32:]
        turned = pltpu.roll(lx, 64, 1)
        xl[0, 18 + t] = lx
        xl[0, t] = turned
        res = dot_t(left1, spread[t])
        lo = res[:32] + res[32:]
        xl[1, 9 + t] = jnp.where(first_half, lo, 0.0)
        xl[1, 18 + t] = jnp.where(first_half, 0.0, lo)
        lhalo_out[t] = (turned * is_first + lo * is_last).astype(BF16)
    lhalo = remote(lhalo_out, lhalo_in, lhalo_sem.at[0], lhalo_sem.at[1], other_half)
    lhalo.start()
    own_group = div(z, 4)
    lane16 = lax.broadcasted_iota(jnp.int32, (16, 128), 1) >> 5

    def spread_panels(g):
        opposite = own_group == (g + 2) % 4

        @pl.when(opposite)
        def _():
            rz.arrived(4, 2 + g)

        @pl.when(jnp.logical_not(opposite))
        def _():
            rz.arrived(3, 2 + g)

        four = [rtiles[4 * g + v].astype(F32) for v in range(4)]
        for layer in range(2):
            piece = jnp.zeros((16, 128), F32)
            for v in range(4):
                shift = (32 * (v - layer)) % 128
                moved = pltpu.roll(four[v], shift, 1) if shift else four[v]
                piece = jnp.where(lane16 == v, moved, piece)
            rall[g, layer, pl.ds(chip, 1)] = piece.astype(BF16)[None]
        for layer in (1, 0):
            for dx, dy in plane:
                part = rall.at[g, layer, chip]
                kind = 2 + layer if g == 2 else 1
                remote(part, part, rp_sem.at[0], rp_sem.at[kind], at(dx, dy)).start()

    for g in (0, 1, 3):
        spread_panels(g)
    act.forward()
    spread_panels(2)
    for d in (4, 12):
        share(d).start()
    act.arrived(6, 2)
    for d in (1, 15, 2, 14, 3, 13):
        share(d).start()

    for t in range(9):
        res = dot_t(left0, patches[0, t])
        xl[0, 9 + t] = res[:32] + res[32:]

    fetch[9].wait()
    big_row = lax.broadcasted_iota(jnp.int32, (256, 256), 0)
    big_col = lax.broadcasted_iota(jnp.int32, (256, 256), 1)
    same = (big_row & 7) == (big_col & 7)
    er = lax.broadcasted_iota(jnp.int32, (256, 32), 0)
    ec = lax.broadcasted_iota(jnp.int32, (256, 32), 1)
    expand = jnp.where((er >> 3) == ec, 1.0, 0.0).astype(BF16)
    mixpad[...] = jnp.zeros((2, 32, 32), F32)
    wide = []
    for layer in range(2):
        mixpad[layer, 0:27, 0:27] = mix_ref[:, layer, :]
        for part in split(mixpad[layer]):
            tall = dot(expand, part).astype(BF16)
            wide.append(jnp.where(same, dot_t(tall, expand), 0.0).astype(BF16))

    lhalo.wait_recv()
    for t in range(9):
        edge = lhalo_in[t].astype(F32)
        xl[0, t] = jnp.where(first_half, edge * is_last, xl[0, t])
        xl[1, t] = jnp.where(first_half, 0.0, edge * is_first)
    mc = {}
    for layer in (1, 0):
        for t in range(27, 32):
            xl[layer, t] = jnp.zeros((32, 128), F32)
        block = jnp.concatenate(
            [xl[layer, :, 8 * q : 8 * q + 8, :].reshape(256, 128) for q in range(4)], axis=1
        )
        high, low = split(block)
        res = dot(wide[2 * layer], high) + dot(wide[2 * layer], low) + dot(wide[2 * layer + 1], high)
        for q in range(4):
            mixed32[:, 8 * q : 8 * q + 8, :] = res[:, 128 * q : 128 * q + 128].reshape(32, 8, 128)
        mixed[layer] = mixed32[0:28].reshape(COLS, 128).astype(BF16)
        mc[layer] = remote(
            mixed.at[layer], mixed_far.at[layer], mc_sem.at[2], mc_sem.at[layer], other_core
        )
        mc[layer].start()

    for d in (5, 11, 6, 10, 7, 9, 8):
        act.arrived(1, d - 2)
        share(d).start()
    everything = remote(acts, acts_far, cf_sem.at[0], cf_sem.at[1], other_core)
    everything.wait_recv()

    first = {0: xi, 1: y}
    second = {0: y, 1: xi}
    offs = (2, 1, 3, 0)

    def along(layer, step):
        return at(step, 0) if layer == 0 else at(0, step)

    def across(layer, step):
        return at(0, step) if layer == 0 else at(step, 0)

    def columns(k, n):
        cut = 512 if k < 2 else 384
        return slice(0, cut) if n in (0, 3, 4) else slice(cut, COLS)

    def send1(layer, k, n):
        step = 1 if n in (0, 2, 4) else 3
        cols = columns(k, n)
        width = slice(0, cols.stop - cols.start)
        return remote(
            p1_send.at[layer, k, n, :, width], p1_in.at[layer, k, n, :, width],
            p1_ssem.at[0], p1_rsem.at[layer, k, 0 if n < 2 else 1], along(layer, step),
        )

    def arrived1(layer, k, late):
        rows = s2_in.at[0, pl.ds(0, 1 + late)]
        remote(rows, rows, p1_ssem.at[0], p1_rsem.at[layer, k, late], along(layer, 1)).wait_recv()

    def partial(layer, k, off, cols):
        f, g = rem(first[layer] + off, 4), rem(second[layer] + offs[k], 4)
        return u[layer, pl.ds(f, 1), pl.ds(g, 1), :, cols][0, 0]

    def got(layer, k, n):
        cols = columns(k, n)
        return p1_in[layer, k, n, :, : cols.stop - cols.start].astype(F32)

    def put(layer, k, n, value):
        cols = columns(k, n)
        p1_send[layer, k, n, :, : cols.stop - cols.start] = value.astype(BF16)
        send1(layer, k, n).start()

    def panels(part, kind):
        return remote(part, part, rp_sem.at[0], rp_sem.at[kind], at(1, 0))

    some = pl.ds(0, NX * NY - 1)
    panels(rall.at[pl.ds(0, 3), :, some], 1).wait_recv()
    for layer in (1, 0):
        mc[layer].wait_recv()
        panels(rall.at[2, layer, some], 2 + layer).wait_recv()
        rows = pl.ds(0, 32) if layer == 1 else pl.ds(32, 32)
        both = jnp.concatenate(
            [acts[:, rows, :].reshape(512, 128), acts_far[:, rows, :].reshape(512, 128)], axis=1
        )
        panel = jnp.concatenate([rall[g, layer].reshape(256, 128) for g in range(4)], axis=1)
        turned_act = dot(panel, both)
        high, low = split(turned_act)
        mix = jnp.concatenate([mixed[layer], mixed_far[layer]], axis=1)
        res = dot_t(high, mix) + dot_t(low, mix)
        for a in range(4):
            for b in range(4):
                spot = (a, b) if layer == 0 else (b, a)
                u[(layer, *spot)] = res[(a * 4 + b) * 16 : (a * 4 + b + 1) * 16]
        for k in range(4):
            for n in (0, 1):
                put(layer, k, n, partial(layer, k, 2, columns(k, n)))
        for k in range(4):
            put(layer, k, 2, partial(layer, k, 1, columns(k, 2)))
            put(layer, k, 3, partial(layer, k, 3, columns(k, 3)))

    halo.wait_send()
    lhalo.wait_send()
    rz.sent()
    act.sent()
    everything.wait_send()
    panels(rall.at[:, :, some], 1).wait_send()
    remote(mixed, mixed_far, mc_sem.at[2], mc_sem.at[0], other_core).wait_send()

    for k in range(4):
        for layer in (1, 0):
            arrived1(layer, k, 0)
            put(layer, k, 4, partial(layer, k, 1, columns(k, 4)) + got(layer, k, 0))
            put(layer, k, 5, partial(layer, k, 3, columns(k, 5)) + got(layer, k, 1))
    kept = {}
    for k in range(4):
        for layer in (1, 0):
            arrived1(layer, k, 1)
            left = partial(layer, k, 0, columns(k, 4)) + got(layer, k, 3) + got(layer, k, 4)
            right = partial(layer, k, 0, columns(k, 5)) + got(layer, k, 2) + got(layer, k, 5)
            total = jnp.concatenate([left, right], axis=1)
            d = offs[k]
            if d == 0:
                kept[layer] = total
                continue
            s2_send[layer, d - 1] = total.astype(BF16)
            remote(
                s2_send.at[layer, d - 1], s2_in.at[layer, d - 1],
                p2_sem.at[2], p2_sem.at[layer], across(layer, d),
            ).start()
    for layer in (1, 0):
        total = kept[layer]
        remote(
            s2_send.at[layer], s2_in.at[layer], p2_sem.at[2], p2_sem.at[layer], across(layer, 1)
        ).wait_recv()
        for d in (1, 3, 2):
            total = total + s2_in[layer, d - 1].astype(F32)
        for s in range(TAPS):
            out_ref[layer, s] = total[:, 32 * s : 32 * s + 32].astype(BF16)

    rows = u.at[0, pl.ds(0, 3)]
    remote(rows, rows, p1_ssem.at[0], p1_rsem.at[0, 0, 0], along(0, 1)).wait_send()
    remote(s2_send, s2_in, p2_sem.at[2], p2_sem.at[0], across(0, 1)).wait_send()


def shards(clip_input, first_kernel, second_kernel, out_grad, tap_mix, left_panels, right_panels):
    vmem = pltpu.VMEM
    dma = pltpu.SemaphoreType.DMA
    operands = (
        clip_input.reshape(4, 256, 512),
        first_kernel.swapaxes(1, 2),
        second_kernel,
        out_grad.reshape(4, 4, 512),
        tap_mix.swapaxes(0, 1),
        left_panels,
        right_panels.swapaxes(1, 2),
    )
    out = pl.pallas_call(
        kernel,
        name="shampoo_update",
        out_shape=jax.ShapeDtypeStruct((2, TAPS, 16, 32), BF16),
        in_specs=[pl.BlockSpec(memory_space=pl.ANY)] * len(operands),
        out_specs=pl.BlockSpec(memory_space=pltpu.VMEM),
        scratch_shapes=[
            *(vmem(v.shape, v.dtype) for v in operands),
            vmem((2, 9, 128, 512), BF16),
            vmem((9, 128, 512), BF16),
            vmem((16, 512), F32),
            vmem((32, 128), F32),
            vmem((32, 128), F32),
            vmem((9, 32, 128), BF16),
            vmem((9, 32, 128), BF16),
            vmem((NZ, 64, 128), BF16),
            vmem((NZ, 64, 128), BF16),
            vmem((NZ, 16, 128), BF16),
            vmem((4, 2, NX * NY, 16, 128), BF16),
            vmem((2, 32, 32, 128), F32),
            vmem((32, 32, 128), F32),
            vmem((2, COLS, 128), BF16),
            vmem((2, COLS, 128), BF16),
            vmem((2, 32, 32), F32),
            vmem((2, 4, 4, 16, COLS), F32),
            vmem((2, 4, 6, 16, 512), BF16),
            vmem((2, 4, 6, 16, 512), BF16),
            vmem((2, 3, 16, COLS), BF16),
            vmem((2, 3, 16, COLS), BF16),
            dma((10,)), dma((2,)), dma((2,)),
            dma((1,)), dma((10,)), dma((1,)), dma((6,)),
            dma((4,)), dma((2,)), dma((3,)), dma((1,)), dma((2, 4, 2)), dma((3,)),
        ],
        compiler_params=pltpu.CompilerParams(collective_id=0, has_side_effects=True),
    )(*operands)
    return out.swapaxes(2, 3)


def solution(mesh):
    in_specs = (
        P("replica", "tm", None, None, None),
        P(None, None, "fsdp"),
        P(None, "fsdp", None),
        P("replica", "tm", None, None, None),
        P(),
        P(None, "fsdp", None),
        P(None, "fsdp", ("replica", "tm")),
    )
    out_specs = P(None, None, "fsdp", ("replica", "tm"))
    return jax.shard_map(shards, mesh=mesh, in_specs=in_specs, out_specs=out_specs, check_vma=False)
```

```python
import jax
import jax.numpy as jnp
from jax import lax
from jax.experimental import pallas as pl
from jax.experimental.pallas import tpu as pltpu
from jax.sharding import PartitionSpec as P

TAPS = 27
MESH = pl.DeviceIdType.MESH
F32 = jnp.float32
BF16 = jnp.bfloat16
NZ = 16
NX = 4
NY = 4
COLS = 896


def rem(a, n):
    return lax.rem(a, jnp.int32(n))


def div(a, n):
    return lax.div(a, jnp.int32(n))


def dot(a, b):
    return lax.dot_general(a, b, (((1,), (0,)), ((), ())), preferred_element_type=F32)


def dot_t(a, b):
    return lax.dot_general(a, b, (((1,), (1,)), ((), ())), preferred_element_type=F32)


def split(v):
    high = v.astype(BF16)
    return high, (v - high.astype(F32)).astype(BF16)


def gather_rows(b, c, rows, wide):
    shape = (64, wide * wide)
    position = lax.broadcasted_iota(jnp.int32, shape, 0)
    cell = lax.broadcasted_iota(jnp.int32, shape, 1)
    yh, xh = position >> 3, position & 7
    if rows == "read":
        hit = cell == (2 * yh + (b - 1)) * wide + 2 * xh + (c - 1)
        if c == 0:
            hit = hit & (xh > 0)
    else:
        yq, xq = cell >> 2, cell & 3
        hit = (yh == 2 * yq + (b - 1)) & (xh == 2 * xq + (c - 1))
    return jnp.where(hit, 1.0, 0.0).astype(BF16)


def kernel(
    x_hbm, k1_hbm, k2_hbm, og_hbm, mix_hbm, left_hbm, right_hbm, out_ref,
    x_ref, k1_ref, k2_ref, og_ref, mix_ref, left_ref, right_ref,
    patches, spread, og_wide, halo_out, halo_in, lhalo_out, lhalo_in,
    acts, acts_far, rtiles, rall, xl, mixed32, mixed, mixed_far, mixpad,
    u, p1_send, p1_in, s2_send, s2_in,
    in_sem, halo_sem, lhalo_sem, act_ssem, act_rsem, rz_ssem, rz_rsem,
    rp_sem, cf_sem, mc_sem, p1_ssem, p1_rsem, p2_sem,
):
    z = lax.axis_index("fsdp")
    rep = lax.axis_index("replica")
    tm = lax.axis_index("tm")
    core = rem(rep, 2)
    y = rem(div(rep, 2), NY)
    x_lo = div(rep, 2 * NY)
    xi = tm * 2 + x_lo
    chip = xi * NY + y

    x_at = [rem(xi + d, NX) for d in range(NX)]
    x_part = [(rem(v, 2) * 2 * NY, div(v, 2)) for v in x_at]
    y_part = [rem(y + d, NY) * 2 + core for d in range(NY)]
    plane = [(dx, dy) for dx in (2, 1, 3, 0) for dy in (2, 1, 3, 0) if dx or dy]

    def at(dx, dy):
        return {"replica": x_part[dx][0] + y_part[dy], "tm": x_part[dx][1]}

    def up(d):
        return rem(z + d, NZ)

    def remote(src, dst, ssem, rsem, device):
        return pltpu.make_async_remote_copy(
            src_ref=src, dst_ref=dst, send_sem=ssem, recv_sem=rsem,
            device_id=device, device_id_type=MESH,
        )

    other_core = {"replica": rep + 1 - 2 * core}
    other_half = {"tm": 1 - tm}

    fetch = [
        pltpu.make_async_copy(src, dst, in_sem.at[n])
        for n, (src, dst) in enumerate(
            [(x_hbm.at[f], x_ref.at[f]) for f in range(4)]
            + [
                (right_hbm, right_ref), (left_hbm, left_ref), (k1_hbm, k1_ref),
                (og_hbm, og_ref), (k2_hbm, k2_ref), (mix_hbm, mix_ref),
            ]
        )
    ]
    for n in (1, 3, 6):
        fetch[n].start()

    barrier = pltpu.get_barrier_semaphore()

    def greet(device):
        pl.semaphore_signal(barrier, inc=1, device_id=device, device_id_type=MESH)

    for d in (4, 12, 3, 13, 2, 14, 1, 15):
        greet({"fsdp": up(d)})

    for dx, dy in plane:
        greet(at(dx, dy))
    greet(other_core)
    for n in (7, 8, 4, 0, 2, 5, 9):
        fetch[n].start()

    lane = lax.broadcasted_iota(jnp.int32, (32, 128), 1)
    first_half = lane < 64
    is_first = jnp.where(tm == 0, 1.0, 0.0).astype(F32)
    is_last = 1.0 - is_first

    select = jnp.concatenate([gather_rows(t // 3, t % 3, "read", 16) for t in range(9)], axis=0)

    def pick(pair, frames):
        for slot, frame in enumerate(frames):
            fetch[frame].wait()
            picked = dot(select, x_ref[frame]).astype(BF16)
            for t in range(9):
                patches[pair, t, slot * 64 : (slot + 1) * 64, :] = picked[t * 64 : (t + 1) * 64]

    pick(1, (1, 3))
    fetch[6].wait()
    odd = jnp.zeros((64, 128), F32)
    for t in range(9):
        odd = odd + dot_t(jnp.concatenate([k1_ref[t], k1_ref[18 + t]], axis=0), patches[1, t])
    turned_pre = pltpu.roll(odd[:32], 64, 1)

    fetch[4].wait()
    row = lax.broadcasted_iota(jnp.int32, (32, 128), 0)
    tile = dot(right_ref[0].astype(BF16), jnp.where(lane == row, 1.0, 0.0).astype(BF16))
    tile = tile + dot(right_ref[1].astype(BF16), jnp.where(lane == row + 32, 1.0, 0.0).astype(BF16))
    tile = tile[:8] + pltpu.roll(tile[8:], 64, 1)
    rtiles[pl.ds(z, 1)] = tile.astype(BF16)[None]

    even_z = rem(z, 2) == 0

    class Ring:
        def __init__(self, buf, ssem, rsem, group):
            self.buf, self.ssem, self.rsem, self.group = buf, ssem, rsem, group

        def copy(self, back, d):
            block = up(NZ - back)
            gap = (back + d) % NZ
            kind = {4: 0, 12: 1}.get(gap)
            kind = self.group(block, gap) if kind is None else kind
            return remote(
                self.buf.at[block], self.buf.at[block], self.ssem.at[0], self.rsem.at[kind],
                {"fsdp": up(d)},
            )

        def start(self):
            for e in (4, 3, 2, 1):
                self.copy(0, e).start()
                self.copy(0, NZ - e).start()

        def arrived(self, count, kind):
            part = self.buf.at[pl.ds(0, count)]
            remote(part, part, self.ssem.at[0], self.rsem.at[kind], {"fsdp": up(1)}).wait_recv()

        def forward(self):
            self.arrived(1, 0)

            @pl.when(even_z)
            def _():
                self.copy(4, 4).start()

            for k in (3, 2, 1):
                self.copy(4, k).start()
            self.arrived(1, 1)

            @pl.when(jnp.logical_not(even_z))
            def _():
                self.copy(12, NZ - 4).start()

            for k in (3, 2, 1):
                self.copy(12, NZ - k).start()

        def sent(self):
            part = self.buf.at[pl.ds(0, NZ - 1)]
            remote(part, part, self.ssem.at[0], self.rsem.at[0], {"fsdp": up(1)}).wait_send()

    rz = Ring(rtiles, rz_ssem, rz_rsem, lambda block, gap: 2 + div(block, 4))
    act = Ring(acts, act_ssem, act_rsem, lambda block, gap: gap - 2 if 4 < gap < 12 else 2)
    place = jnp.concatenate([gather_rows(t // 3, t % 3, "spread", 4) for t in range(9)], axis=0)
    fetch[7].wait()
    for r in range(4):
        og_wide[4 * r : 4 * r + 4, :] = og_ref[r].astype(F32)
    picked = dot(place, og_wide[...].astype(BF16)).astype(BF16)
    for t in range(9):
        spread[t, :64, :] = picked[t * 64 : (t + 1) * 64]
        spread[t, 64:, :] = picked[t * 64 : (t + 1) * 64]
    fetch[8].wait()
    back = jnp.zeros((96, 128), F32)
    for t in range(9):
        stack = jnp.concatenate([k2_ref[t], k2_ref[9 + t], k2_ref[18 + t]], axis=0)
        back = back + dot_t(stack, spread[t])
    halo_out[...] = turned_pre * is_first + back[:32] * is_last

    pl.semaphore_wait(barrier, 8 + NX * NY - 1 + 1)

    halo = remote(halo_out, halo_in, halo_sem.at[0], halo_sem.at[1], other_half)
    halo.start()
    rz.start()

    pick(0, (0, 2))
    even = jnp.zeros((32, 128), F32)
    for t in range(9):
        even = even + dot_t(k1_ref[9 + t], patches[0, t])

    rz.forward()

    halo.wait_recv()
    received = halo_in[...]
    pre = even + odd[32:] + jnp.where(first_half, received * is_last, turned_pre)
    hidden_grad = jnp.where(first_half, back[32:64], back[64:96] + received * is_first)
    sig = jax.nn.sigmoid(pre)
    hidden = pre * sig
    pre_grad = hidden_grad * sig * (1.0 + pre * (1.0 - sig))
    acts[pl.ds(z, 1)] = jnp.concatenate([hidden, pre_grad], axis=0).astype(BF16)[None]
    act.start()

    def share(d):
        block = up(NZ - d)
        return remote(acts.at[block], acts_far.at[block], cf_sem.at[0], cf_sem.at[1], other_core)

    share(0).start()

    fetch[5].wait()
    left0 = jnp.concatenate(split(left_ref[0]), axis=0)
    left1 = jnp.concatenate(split(left_ref[1]), axis=0)
    for t in range(9):
        res = dot_t(left0, patches[1, t])
        lx = res[:32] + res[32:]
        turned = pltpu.roll(lx, 64, 1)
        xl[0, 18 + t] = lx
        xl[0, t] = turned
        res = dot_t(left1, spread[t])
        lo = res[:32] + res[32:]
        xl[1, 9 + t] = jnp.where(first_half, lo, 0.0)
        xl[1, 18 + t] = jnp.where(first_half, 0.0, lo)
        lhalo_out[t] = (turned * is_first + lo * is_last).astype(BF16)
    lhalo = remote(lhalo_out, lhalo_in, lhalo_sem.at[0], lhalo_sem.at[1], other_half)
    lhalo.start()
    own_group = div(z, 4)
    lane16 = lax.broadcasted_iota(jnp.int32, (16, 128), 1) >> 5

    def spread_panels(g):
        opposite = own_group == (g + 2) % 4

        @pl.when(opposite)
        def _():
            rz.arrived(4, 2 + g)

        @pl.when(jnp.logical_not(opposite))
        def _():
            rz.arrived(3, 2 + g)

        four = [rtiles[4 * g + v].astype(F32) for v in range(4)]
        four = [jnp.concatenate([v, pltpu.roll(v, 64, 1)], axis=0) for v in four]
        for layer in range(2):
            piece = jnp.zeros((16, 128), F32)
            for v in range(4):
                shift = (32 * (v - layer)) % 128
                moved = pltpu.roll(four[v], shift, 1) if shift else four[v]
                piece = jnp.where(lane16 == v, moved, piece)
            rall[g, layer, pl.ds(chip, 1)] = piece.astype(BF16)[None]
        for layer in (1, 0):
            for dx, dy in plane:
                part = rall.at[g, layer, chip]
                kind = 2 + layer if g == 2 else 1
                remote(part, part, rp_sem.at[0], rp_sem.at[kind], at(dx, dy)).start()

    for g in (0, 1, 3):
        spread_panels(g)
    act.forward()
    spread_panels(2)
    for d in (4, 12):
        share(d).start()
    act.arrived(6, 2)
    for d in (1, 15, 2, 14, 3, 13):
        share(d).start()

    for t in range(9):
        res = dot_t(left0, patches[0, t])
        xl[0, 9 + t] = res[:32] + res[32:]

    fetch[9].wait()
    big_row = lax.broadcasted_iota(jnp.int32, (256, 256), 0)
    big_col = lax.broadcasted_iota(jnp.int32, (256, 256), 1)
    same = (big_row & 7) == (big_col & 7)
    er = lax.broadcasted_iota(jnp.int32, (256, 32), 0)
    ec = lax.broadcasted_iota(jnp.int32, (256, 32), 1)
    expand = jnp.where((er >> 3) == ec, 1.0, 0.0).astype(BF16)
    mixpad[...] = jnp.zeros((2, 32, 32), F32)
    wide = []
    for layer in range(2):
        mixpad[layer, 0:27, 0:27] = mix_ref[:, layer, :]
        for part in split(mixpad[layer]):
            tall = dot(expand, part).astype(BF16)
            wide.append(jnp.where(same, dot_t(tall, expand), 0.0).astype(BF16))

    lhalo.wait_recv()
    for t in range(9):
        edge = lhalo_in[t].astype(F32)
        xl[0, t] = jnp.where(first_half, edge * is_last, xl[0, t])
        xl[1, t] = jnp.where(first_half, 0.0, edge * is_first)
    mc = {}
    for layer in (1, 0):
        for t in range(27, 32):
            xl[layer, t] = jnp.zeros((32, 128), F32)
        block = jnp.concatenate(
            [xl[layer, :, 8 * q : 8 * q + 8, :].reshape(256, 128) for q in range(4)], axis=1
        )
        high, low = split(block)
        res = dot(wide[2 * layer], high) + dot(wide[2 * layer], low) + dot(wide[2 * layer + 1], high)
        for q in range(4):
            mixed32[:, 8 * q : 8 * q + 8, :] = res[:, 128 * q : 128 * q + 128].reshape(32, 8, 128)
        mixed[layer] = mixed32[0:28].reshape(COLS, 128).astype(BF16)
        mc[layer] = remote(
            mixed.at[layer], mixed_far.at[layer], mc_sem.at[2], mc_sem.at[layer], other_core
        )
        mc[layer].start()

    for d in (5, 11, 6, 10, 7, 9, 8):
        act.arrived(1, d - 2)
        share(d).start()
    everything = remote(acts, acts_far, cf_sem.at[0], cf_sem.at[1], other_core)
    everything.wait_recv()

    first = {0: xi, 1: y}
    second = {0: y, 1: xi}
    offs = (2, 1, 3, 0)

    def along(layer, step):
        return at(step, 0) if layer == 0 else at(0, step)

    def across(layer, step):
        return at(0, step) if layer == 0 else at(step, 0)

    def columns(k, n):
        cut = 512 if k < 2 else 384
        return slice(0, cut) if n in (0, 3, 4) else slice(cut, COLS)

    def send1(layer, k, n):
        step = 1 if n in (0, 2, 4) else 3
        cols = columns(k, n)
        width = slice(0, cols.stop - cols.start)
        return remote(
            p1_send.at[layer, k, n, :, width], p1_in.at[layer, k, n, :, width],
            p1_ssem.at[0], p1_rsem.at[layer, k, 0 if n < 2 else 1], along(layer, step),
        )

    def arrived1(layer, k, late):
        rows = s2_in.at[0, pl.ds(0, 1 + late)]
        remote(rows, rows, p1_ssem.at[0], p1_rsem.at[layer, k, late], along(layer, 1)).wait_recv()

    def partial(layer, k, off, cols):
        f, g = rem(first[layer] + off, 4), rem(second[layer] + offs[k], 4)
        return u[layer, pl.ds(f, 1), pl.ds(g, 1), :, cols][0, 0]

    def got(layer, k, n):
        cols = columns(k, n)
        return p1_in[layer, k, n, :, : cols.stop - cols.start].astype(F32)

    def put(layer, k, n, value):
        cols = columns(k, n)
        p1_send[layer, k, n, :, : cols.stop - cols.start] = value.astype(BF16)
        send1(layer, k, n).start()

    def panels(part, kind):
        return remote(part, part, rp_sem.at[0], rp_sem.at[kind], at(1, 0))

    some = pl.ds(0, NX * NY - 1)
    panels(rall.at[pl.ds(0, 3), :, some], 1).wait_recv()
    operands = {}

    def product(layer, offsets):
        both, mix = operands[layer]
        spots = [rem(first[layer] + off, 4) for off in offsets]
        rows = []
        for f in spots:
            for b in range(4):
                to = f * 4 + b if layer == 0 else b * 4 + f
                rows.append(
                    jnp.concatenate([rall[g, layer, pl.ds(to, 1)][0] for g in range(4)], axis=1)
                )
        high, low = split(dot(jnp.concatenate(rows, axis=0), both))
        res = dot_t(high, mix) + dot_t(low, mix)
        for n, f in enumerate(spots):
            u[layer, pl.ds(f, 1)] = res[64 * n : 64 * n + 64].reshape(1, 4, 16, COLS)

    for layer in (1, 0):
        mc[layer].wait_recv()
        panels(rall.at[2, layer, some], 2 + layer).wait_recv()
        rows = pl.ds(0, 32) if layer == 1 else pl.ds(32, 32)
        both = jnp.concatenate(
            [acts[:, rows, :].reshape(512, 128), acts_far[:, rows, :].reshape(512, 128)], axis=1
        )
        operands[layer] = both, jnp.concatenate([mixed[layer], mixed_far[layer]], axis=1)
        product(layer, (2,))
        for k in range(4):
            for n in (0, 1):
                put(layer, k, n, partial(layer, k, 2, columns(k, n)))
    for layer in (1, 0):
        product(layer, (1, 3, 0))
        for k in range(4):
            put(layer, k, 2, partial(layer, k, 1, columns(k, 2)))
            put(layer, k, 3, partial(layer, k, 3, columns(k, 3)))

    halo.wait_send()
    lhalo.wait_send()
    rz.sent()
    act.sent()
    everything.wait_send()
    panels(rall.at[:, :, some], 1).wait_send()
    remote(mixed, mixed_far, mc_sem.at[2], mc_sem.at[0], other_core).wait_send()

    for k in range(4):
        for layer in (1, 0):
            arrived1(layer, k, 0)
            put(layer, k, 4, partial(layer, k, 1, columns(k, 4)) + got(layer, k, 0))
            put(layer, k, 5, partial(layer, k, 3, columns(k, 5)) + got(layer, k, 1))
    kept = {}
    for k in range(4):
        for layer in (1, 0):
            arrived1(layer, k, 1)
            left = partial(layer, k, 0, columns(k, 4)) + got(layer, k, 3) + got(layer, k, 4)
            right = partial(layer, k, 0, columns(k, 5)) + got(layer, k, 2) + got(layer, k, 5)
            total = jnp.concatenate([left, right], axis=1)
            d = offs[k]
            if d == 0:
                kept[layer] = total
                continue
            s2_send[layer, d - 1] = total.astype(BF16)
            remote(
                s2_send.at[layer, d - 1], s2_in.at[layer, d - 1],
                p2_sem.at[2], p2_sem.at[layer], across(layer, d),
            ).start()
    for layer in (1, 0):
        total = kept[layer]
        remote(
            s2_send.at[layer], s2_in.at[layer], p2_sem.at[2], p2_sem.at[layer], across(layer, 1)
        ).wait_recv()
        for d in (1, 3, 2):
            total = total + s2_in[layer, d - 1].astype(F32)
        for s in range(TAPS):
            out_ref[layer, s] = total[:, 32 * s : 32 * s + 32].astype(BF16)

    rows = u.at[0, pl.ds(0, 3)]
    remote(rows, rows, p1_ssem.at[0], p1_rsem.at[0, 0, 0], along(0, 1)).wait_send()
    remote(s2_send, s2_in, p2_sem.at[2], p2_sem.at[0], across(0, 1)).wait_send()


def shards(clip_input, first_kernel, second_kernel, out_grad, tap_mix, left_panels, right_panels):
    vmem = pltpu.VMEM
    dma = pltpu.SemaphoreType.DMA
    operands = (
        clip_input.reshape(4, 256, 512),
        first_kernel.swapaxes(1, 2),
        second_kernel,
        out_grad.reshape(4, 4, 512),
        tap_mix.swapaxes(0, 1),
        left_panels,
        right_panels.swapaxes(1, 2),
    )
    out = pl.pallas_call(
        kernel,
        name="shampoo_update",
        out_shape=jax.ShapeDtypeStruct((2, TAPS, 16, 32), BF16),
        in_specs=[pl.BlockSpec(memory_space=pl.ANY)] * len(operands),
        out_specs=pl.BlockSpec(memory_space=pltpu.VMEM),
        scratch_shapes=[
            *(vmem(v.shape, v.dtype) for v in operands),
            vmem((2, 9, 128, 512), BF16),
            vmem((9, 128, 512), BF16),
            vmem((16, 512), F32),
            vmem((32, 128), F32),
            vmem((32, 128), F32),
            vmem((9, 32, 128), BF16),
            vmem((9, 32, 128), BF16),
            vmem((NZ, 64, 128), BF16),
            vmem((NZ, 64, 128), BF16),
            vmem((NZ, 8, 128), BF16),
            vmem((4, 2, NX * NY, 16, 128), BF16),
            vmem((2, 32, 32, 128), F32),
            vmem((32, 32, 128), F32),
            vmem((2, COLS, 128), BF16),
            vmem((2, COLS, 128), BF16),
            vmem((2, 32, 32), F32),
            vmem((2, 4, 4, 16, COLS), F32),
            vmem((2, 4, 6, 16, 512), BF16),
            vmem((2, 4, 6, 16, 512), BF16),
            vmem((2, 3, 16, COLS), BF16),
            vmem((2, 3, 16, COLS), BF16),
            dma((10,)), dma((2,)), dma((2,)),
            dma((1,)), dma((10,)), dma((1,)), dma((6,)),
            dma((4,)), dma((2,)), dma((3,)), dma((1,)), dma((2, 4, 2)), dma((3,)),
        ],
        compiler_params=pltpu.CompilerParams(collective_id=0, has_side_effects=True),
    )(*operands)
    return out.swapaxes(2, 3)


def solution(mesh):
    in_specs = (
        P("replica", "tm", None, None, None),
        P(None, None, "fsdp"),
        P(None, "fsdp", None),
        P("replica", "tm", None, None, None),
        P(),
        P(None, "fsdp", None),
        P(None, "fsdp", ("replica", "tm")),
    )
    out_specs = P(None, None, "fsdp", ("replica", "tm"))
    return jax.shard_map(shards, mesh=mesh, in_specs=in_specs, out_specs=out_specs, check_vma=False)
```

```python
import jax
import jax.numpy as jnp
from jax import lax
from jax.experimental import pallas as pl
from jax.experimental.pallas import tpu as pltpu
from jax.sharding import PartitionSpec as P

TAPS = 27
MESH = pl.DeviceIdType.MESH
F32 = jnp.float32
BF16 = jnp.bfloat16
NZ = 16
NX = 4
NY = 4
COLS = 896


def rem(a, n):
    return lax.rem(a, jnp.int32(n))


def div(a, n):
    return lax.div(a, jnp.int32(n))


def dot(a, b):
    return lax.dot_general(a, b, (((1,), (0,)), ((), ())), preferred_element_type=F32)


def dot_t(a, b):
    return lax.dot_general(a, b, (((1,), (1,)), ((), ())), preferred_element_type=F32)


def split(v):
    high = v.astype(BF16)
    return high, (v - high.astype(F32)).astype(BF16)


def gather_rows(b, c, rows, wide):
    shape = (64, wide * wide)
    position = lax.broadcasted_iota(jnp.int32, shape, 0)
    cell = lax.broadcasted_iota(jnp.int32, shape, 1)
    yh, xh = position >> 3, position & 7
    if rows == "read":
        hit = cell == (2 * yh + (b - 1)) * wide + 2 * xh + (c - 1)
        if c == 0:
            hit = hit & (xh > 0)
    else:
        yq, xq = cell >> 2, cell & 3
        hit = (yh == 2 * yq + (b - 1)) & (xh == 2 * xq + (c - 1))
    return jnp.where(hit, 1.0, 0.0).astype(BF16)


def kernel(
    x_hbm, k1_hbm, k2_hbm, og_hbm, mix_hbm, left_hbm, right_hbm, out_ref,
    x_ref, k1_ref, k2_ref, og_ref, mix_ref, left_ref, right_ref,
    patches, spread, og_wide, halo_out, halo_in, lhalo_out, lhalo_in,
    acts, acts_far, rtiles, rall, xl, mixed32, mixed, mixed_far, mixpad,
    u, p1_send, p1_in, s2_send, s2_in,
    in_sem, halo_sem, lhalo_sem, act_ssem, act_rsem, rz_ssem, rz_rsem,
    rp_sem, cf_sem, mc_sem, p1_ssem, p1_rsem, p2_sem,
):
    z = lax.axis_index("fsdp")
    rep = lax.axis_index("replica")
    tm = lax.axis_index("tm")
    core = rem(rep, 2)
    y = rem(div(rep, 2), NY)
    x_lo = div(rep, 2 * NY)
    xi = tm * 2 + x_lo
    chip = xi * NY + y

    x_at = [rem(xi + d, NX) for d in range(NX)]
    x_part = [(rem(v, 2) * 2 * NY, div(v, 2)) for v in x_at]
    y_part = [rem(y + d, NY) * 2 + core for d in range(NY)]
    plane = [(dx, dy) for dx in (2, 1, 3, 0) for dy in (2, 1, 3, 0) if dx or dy]

    def at(dx, dy):
        return {"replica": x_part[dx][0] + y_part[dy], "tm": x_part[dx][1]}

    def up(d):
        return rem(z + d, NZ)

    def remote(src, dst, ssem, rsem, device):
        return pltpu.make_async_remote_copy(
            src_ref=src, dst_ref=dst, send_sem=ssem, recv_sem=rsem,
            device_id=device, device_id_type=MESH,
        )

    other_core = {"replica": rep + 1 - 2 * core}
    other_half = {"tm": 1 - tm}

    fetch = [
        pltpu.make_async_copy(src, dst, in_sem.at[n])
        for n, (src, dst) in enumerate(
            [(x_hbm.at[f], x_ref.at[f]) for f in range(4)]
            + [
                (right_hbm, right_ref), (left_hbm, left_ref), (k1_hbm, k1_ref),
                (og_hbm, og_ref), (k2_hbm, k2_ref), (mix_hbm, mix_ref),
            ]
        )
    ]
    for n in (7, 1, 3, 6):
        fetch[n].start()

    barrier = pltpu.get_barrier_semaphore()

    def greet(device):
        pl.semaphore_signal(barrier, inc=1, device_id=device, device_id_type=MESH)

    for d in (4, 12, 3, 13, 2, 14, 1, 15):
        greet({"fsdp": up(d)})

    for dx, dy in plane:
        greet(at(dx, dy))
    greet(other_core)
    for n in (8, 4, 0, 2, 5, 9):
        fetch[n].start()

    lane = lax.broadcasted_iota(jnp.int32, (32, 128), 1)
    first_half = lane < 64
    is_first = jnp.where(tm == 0, 1.0, 0.0).astype(F32)
    is_last = 1.0 - is_first

    select = jnp.concatenate([gather_rows(t // 3, t % 3, "read", 16) for t in range(9)], axis=0)

    place = jnp.concatenate([gather_rows(t // 3, t % 3, "spread", 4) for t in range(9)], axis=0)
    fetch[7].wait()
    for r in range(4):
        og_wide[4 * r : 4 * r + 4, :] = og_ref[r].astype(F32)
    picked = dot(place, og_wide[...].astype(BF16)).astype(BF16)
    for t in range(9):
        spread[t, :64, :] = picked[t * 64 : (t + 1) * 64]
        spread[t, 64:, :] = picked[t * 64 : (t + 1) * 64]

    def pick(pair, frames):
        for slot, frame in enumerate(frames):
            fetch[frame].wait()
            picked = dot(select, x_ref[frame]).astype(BF16)
            for t in range(9):
                patches[pair, t, slot * 64 : (slot + 1) * 64, :] = picked[t * 64 : (t + 1) * 64]

    pick(1, (1, 3))
    fetch[6].wait()
    odd = jnp.zeros((64, 128), F32)
    for t in range(9):
        odd = odd + dot_t(jnp.concatenate([k1_ref[t], k1_ref[18 + t]], axis=0), patches[1, t])
    turned_pre = pltpu.roll(odd[:32], 64, 1)

    fetch[4].wait()
    row = lax.broadcasted_iota(jnp.int32, (32, 128), 0)
    tile = dot(right_ref[0].astype(BF16), jnp.where(lane == row, 1.0, 0.0).astype(BF16))
    tile = tile + dot(right_ref[1].astype(BF16), jnp.where(lane == row + 32, 1.0, 0.0).astype(BF16))
    tile = tile[:8] + pltpu.roll(tile[8:], 64, 1)
    rtiles[pl.ds(z, 1)] = tile.astype(BF16)[None]

    even_z = rem(z, 2) == 0

    class Ring:
        def __init__(self, buf, ssem, rsem, group):
            self.buf, self.ssem, self.rsem, self.group = buf, ssem, rsem, group

        def copy(self, back, d):
            block = up(NZ - back)
            gap = (back + d) % NZ
            kind = {4: 0, 12: 1}.get(gap)
            kind = self.group(block, gap) if kind is None else kind
            return remote(
                self.buf.at[block], self.buf.at[block], self.ssem.at[0], self.rsem.at[kind],
                {"fsdp": up(d)},
            )

        def start(self):
            for e in (4, 3, 2, 1):
                self.copy(0, e).start()
                self.copy(0, NZ - e).start()

        def arrived(self, count, kind):
            part = self.buf.at[pl.ds(0, count)]
            remote(part, part, self.ssem.at[0], self.rsem.at[kind], {"fsdp": up(1)}).wait_recv()

        def forward(self):
            self.arrived(1, 0)

            @pl.when(even_z)
            def _():
                self.copy(4, 4).start()

            for k in (3, 2, 1):
                self.copy(4, k).start()
            self.arrived(1, 1)

            @pl.when(jnp.logical_not(even_z))
            def _():
                self.copy(12, NZ - 4).start()

            for k in (3, 2, 1):
                self.copy(12, NZ - k).start()

        def sent(self):
            part = self.buf.at[pl.ds(0, NZ - 1)]
            remote(part, part, self.ssem.at[0], self.rsem.at[0], {"fsdp": up(1)}).wait_send()

    rz = Ring(rtiles, rz_ssem, rz_rsem, lambda block, gap: 2 + div(block, 4))
    act = Ring(acts, act_ssem, act_rsem, lambda block, gap: gap - 2 if 4 < gap < 12 else 2)
    fetch[8].wait()
    back = jnp.zeros((96, 128), F32)
    for t in range(9):
        stack = jnp.concatenate([k2_ref[t], k2_ref[9 + t], k2_ref[18 + t]], axis=0)
        back = back + dot_t(stack, spread[t])
    halo_out[...] = turned_pre * is_first + back[:32] * is_last

    pl.semaphore_wait(barrier, 8 + NX * NY - 1 + 1)

    halo = remote(halo_out, halo_in, halo_sem.at[0], halo_sem.at[1], other_half)
    halo.start()
    rz.start()

    pick(0, (0, 2))
    even = jnp.zeros((32, 128), F32)
    for t in range(9):
        even = even + dot_t(k1_ref[9 + t], patches[0, t])

    rz.forward()

    halo.wait_recv()
    received = halo_in[...]
    pre = even + odd[32:] + jnp.where(first_half, received * is_last, turned_pre)
    hidden_grad = jnp.where(first_half, back[32:64], back[64:96] + received * is_first)
    sig = jax.nn.sigmoid(pre)
    hidden = pre * sig
    pre_grad = hidden_grad * sig * (1.0 + pre * (1.0 - sig))
    acts[pl.ds(z, 1)] = jnp.concatenate([hidden, pre_grad], axis=0).astype(BF16)[None]
    act.start()

    def share(d):
        block = up(NZ - d)
        return remote(acts.at[block], acts_far.at[block], cf_sem.at[0], cf_sem.at[1], other_core)

    share(0).start()

    fetch[5].wait()
    left0 = jnp.concatenate(split(left_ref[0]), axis=0)
    left1 = jnp.concatenate(split(left_ref[1]), axis=0)
    for t in range(9):
        res = dot_t(left0, patches[1, t])
        lx = res[:32] + res[32:]
        turned = pltpu.roll(lx, 64, 1)
        xl[0, 18 + t] = lx
        xl[0, t] = turned
        res = dot_t(left1, spread[t])
        lo = res[:32] + res[32:]
        xl[1, 9 + t] = jnp.where(first_half, lo, 0.0)
        xl[1, 18 + t] = jnp.where(first_half, 0.0, lo)
        lhalo_out[t] = (turned * is_first + lo * is_last).astype(BF16)
    lhalo = remote(lhalo_out, lhalo_in, lhalo_sem.at[0], lhalo_sem.at[1], other_half)
    lhalo.start()
    own_group = div(z, 4)
    lane16 = lax.broadcasted_iota(jnp.int32, (16, 128), 1) >> 5

    def spread_panels(g):
        opposite = own_group == (g + 2) % 4

        @pl.when(opposite)
        def _():
            rz.arrived(4, 2 + g)

        @pl.when(jnp.logical_not(opposite))
        def _():
            rz.arrived(3, 2 + g)

        four = [rtiles[4 * g + v].astype(F32) for v in range(4)]
        four = [jnp.concatenate([v, pltpu.roll(v, 64, 1)], axis=0) for v in four]
        for layer in range(2):
            piece = jnp.zeros((16, 128), F32)
            for v in range(4):
                shift = (32 * (v - layer)) % 128
                moved = pltpu.roll(four[v], shift, 1) if shift else four[v]
                piece = jnp.where(lane16 == v, moved, piece)
            rall[g, layer, pl.ds(chip, 1)] = piece.astype(BF16)[None]
        for layer in (1, 0):
            for dx, dy in plane:
                part = rall.at[g, layer, chip]
                kind = 2 + layer if g == 2 else 1
                remote(part, part, rp_sem.at[0], rp_sem.at[kind], at(dx, dy)).start()

    for g in (0, 1, 3):
        spread_panels(g)
    act.forward()
    spread_panels(2)
    for d in (4, 12):
        share(d).start()
    act.arrived(6, 2)
    for d in (1, 15, 2, 14, 3, 13):
        share(d).start()

    for t in range(9):
        res = dot_t(left0, patches[0, t])
        xl[0, 9 + t] = res[:32] + res[32:]

    fetch[9].wait()
    big_row = lax.broadcasted_iota(jnp.int32, (256, 256), 0)
    big_col = lax.broadcasted_iota(jnp.int32, (256, 256), 1)
    same = (big_row & 7) == (big_col & 7)
    er = lax.broadcasted_iota(jnp.int32, (256, 32), 0)
    ec = lax.broadcasted_iota(jnp.int32, (256, 32), 1)
    expand = jnp.where((er >> 3) == ec, 1.0, 0.0).astype(BF16)
    mixpad[...] = jnp.zeros((2, 32, 32), F32)
    wide = []
    for layer in range(2):
        mixpad[layer, 0:27, 0:27] = mix_ref[:, layer, :]
        for part in split(mixpad[layer]):
            tall = dot(expand, part).astype(BF16)
            wide.append(jnp.where(same, dot_t(tall, expand), 0.0).astype(BF16))

    lhalo.wait_recv()
    for t in range(9):
        edge = lhalo_in[t].astype(F32)
        xl[0, t] = jnp.where(first_half, edge * is_last, xl[0, t])
        xl[1, t] = jnp.where(first_half, 0.0, edge * is_first)
    mc = {}
    for layer in (1, 0):
        for t in range(27, 32):
            xl[layer, t] = jnp.zeros((32, 128), F32)
        block = jnp.concatenate(
            [xl[layer, :, 8 * q : 8 * q + 8, :].reshape(256, 128) for q in range(4)], axis=1
        )
        high, low = split(block)
        res = dot(wide[2 * layer], high) + dot(wide[2 * layer], low) + dot(wide[2 * layer + 1], high)
        for q in range(4):
            mixed32[:, 8 * q : 8 * q + 8, :] = res[:, 128 * q : 128 * q + 128].reshape(32, 8, 128)
        mixed[layer] = mixed32[0:28].reshape(COLS, 128).astype(BF16)
        mc[layer] = remote(
            mixed.at[layer], mixed_far.at[layer], mc_sem.at[2], mc_sem.at[layer], other_core
        )
        mc[layer].start()

    for d in (5, 11, 6, 10, 7, 9, 8):
        act.arrived(1, d - 2)
        share(d).start()
    everything = remote(acts, acts_far, cf_sem.at[0], cf_sem.at[1], other_core)
    everything.wait_recv()

    first = {0: xi, 1: y}
    second = {0: y, 1: xi}
    offs = (2, 1, 3, 0)

    def along(layer, step):
        return at(step, 0) if layer == 0 else at(0, step)

    def across(layer, step):
        return at(0, step) if layer == 0 else at(step, 0)

    def columns(k, n):
        cut = 512 if k < 2 else 384
        return slice(0, cut) if n in (0, 3, 4) else slice(cut, COLS)

    def send1(layer, k, n):
        step = 1 if n in (0, 2, 4) else 3
        cols = columns(k, n)
        width = slice(0, cols.stop - cols.start)
        return remote(
            p1_send.at[layer, k, n, :, width], p1_in.at[layer, k, n, :, width],
            p1_ssem.at[0], p1_rsem.at[layer, k, 0 if n < 2 else 1], along(layer, step),
        )

    def arrived1(layer, k, late):
        rows = s2_in.at[0, pl.ds(0, 1 + late)]
        remote(rows, rows, p1_ssem.at[0], p1_rsem.at[layer, k, late], along(layer, 1)).wait_recv()

    def partial(layer, k, off, cols):
        f, g = rem(first[layer] + off, 4), rem(second[layer] + offs[k], 4)
        return u[layer, pl.ds(f, 1), pl.ds(g, 1), :, cols][0, 0]

    def got(layer, k, n):
        cols = columns(k, n)
        return p1_in[layer, k, n, :, : cols.stop - cols.start].astype(F32)

    def put(layer, k, n, value):
        cols = columns(k, n)
        p1_send[layer, k, n, :, : cols.stop - cols.start] = value.astype(BF16)
        send1(layer, k, n).start()

    def panels(part, kind):
        return remote(part, part, rp_sem.at[0], rp_sem.at[kind], at(1, 0))

    some = pl.ds(0, NX * NY - 1)
    panels(rall.at[pl.ds(0, 3), :, some], 1).wait_recv()
    operands = {}

    def product(layer, offsets):
        both, mix = operands[layer]
        spots = [rem(first[layer] + off, 4) for off in offsets]
        rows = []
        for f in spots:
            for b in range(4):
                to = f * 4 + b if layer == 0 else b * 4 + f
                rows.append(
                    jnp.concatenate([rall[g, layer, pl.ds(to, 1)][0] for g in range(4)], axis=1)
                )
        high, low = split(dot(jnp.concatenate(rows, axis=0), both))
        res = dot_t(high, mix) + dot_t(low, mix)
        for n, f in enumerate(spots):
            u[layer, pl.ds(f, 1)] = res[64 * n : 64 * n + 64].reshape(1, 4, 16, COLS)

    for layer in (1, 0):
        mc[layer].wait_recv()
        panels(rall.at[2, layer, some], 2 + layer).wait_recv()
        rows = pl.ds(0, 32) if layer == 1 else pl.ds(32, 32)
        both = jnp.concatenate(
            [acts[:, rows, :].reshape(512, 128), acts_far[:, rows, :].reshape(512, 128)], axis=1
        )
        operands[layer] = both, jnp.concatenate([mixed[layer], mixed_far[layer]], axis=1)
        product(layer, (2,))
        for k in range(4):
            for n in (0, 1):
                put(layer, k, n, partial(layer, k, 2, columns(k, n)))
    for layer in (1, 0):
        product(layer, (1, 3, 0))
        for k in range(4):
            put(layer, k, 2, partial(layer, k, 1, columns(k, 2)))
            put(layer, k, 3, partial(layer, k, 3, columns(k, 3)))

    halo.wait_send()
    lhalo.wait_send()
    rz.sent()
    act.sent()
    everything.wait_send()
    panels(rall.at[:, :, some], 1).wait_send()
    remote(mixed, mixed_far, mc_sem.at[2], mc_sem.at[0], other_core).wait_send()

    for k in range(4):
        for layer in (1, 0):
            arrived1(layer, k, 0)
            put(layer, k, 4, partial(layer, k, 1, columns(k, 4)) + got(layer, k, 0))
            put(layer, k, 5, partial(layer, k, 3, columns(k, 5)) + got(layer, k, 1))
    kept = {}
    for k in range(4):
        for layer in (1, 0):
            arrived1(layer, k, 1)
            left = partial(layer, k, 0, columns(k, 4)) + got(layer, k, 3) + got(layer, k, 4)
            right = partial(layer, k, 0, columns(k, 5)) + got(layer, k, 2) + got(layer, k, 5)
            total = jnp.concatenate([left, right], axis=1)
            d = offs[k]
            if d == 0:
                kept[layer] = total
                continue
            s2_send[layer, d - 1] = total.astype(BF16)
            remote(
                s2_send.at[layer, d - 1], s2_in.at[layer, d - 1],
                p2_sem.at[2], p2_sem.at[layer], across(layer, d),
            ).start()
    for layer in (1, 0):
        total = kept[layer]
        remote(
            s2_send.at[layer], s2_in.at[layer], p2_sem.at[2], p2_sem.at[layer], across(layer, 1)
        ).wait_recv()
        for d in (1, 3, 2):
            total = total + s2_in[layer, d - 1].astype(F32)
        for s in range(TAPS):
            out_ref[layer, s] = total[:, 32 * s : 32 * s + 32].astype(BF16)

    rows = u.at[0, pl.ds(0, 3)]
    remote(rows, rows, p1_ssem.at[0], p1_rsem.at[0, 0, 0], along(0, 1)).wait_send()
    remote(s2_send, s2_in, p2_sem.at[2], p2_sem.at[0], across(0, 1)).wait_send()


def shards(clip_input, first_kernel, second_kernel, out_grad, tap_mix, left_panels, right_panels):
    vmem = pltpu.VMEM
    dma = pltpu.SemaphoreType.DMA
    operands = (
        clip_input.reshape(4, 256, 512),
        first_kernel.swapaxes(1, 2),
        second_kernel,
        out_grad.reshape(4, 4, 512),
        tap_mix.swapaxes(0, 1),
        left_panels,
        right_panels.swapaxes(1, 2),
    )
    out = pl.pallas_call(
        kernel,
        name="shampoo_update",
        out_shape=jax.ShapeDtypeStruct((2, TAPS, 16, 32), BF16),
        in_specs=[pl.BlockSpec(memory_space=pl.ANY)] * len(operands),
        out_specs=pl.BlockSpec(memory_space=pltpu.VMEM),
        scratch_shapes=[
            *(vmem(v.shape, v.dtype) for v in operands),
            vmem((2, 9, 128, 512), BF16),
            vmem((9, 128, 512), BF16),
            vmem((16, 512), F32),
            vmem((32, 128), F32),
            vmem((32, 128), F32),
            vmem((9, 32, 128), BF16),
            vmem((9, 32, 128), BF16),
            vmem((NZ, 64, 128), BF16),
            vmem((NZ, 64, 128), BF16),
            vmem((NZ, 8, 128), BF16),
            vmem((4, 2, NX * NY, 16, 128), BF16),
            vmem((2, 32, 32, 128), F32),
            vmem((32, 32, 128), F32),
            vmem((2, COLS, 128), BF16),
            vmem((2, COLS, 128), BF16),
            vmem((2, 32, 32), F32),
            vmem((2, 4, 4, 16, COLS), F32),
            vmem((2, 4, 6, 16, 512), BF16),
            vmem((2, 4, 6, 16, 512), BF16),
            vmem((2, 3, 16, COLS), BF16),
            vmem((2, 3, 16, COLS), BF16),
            dma((10,)), dma((2,)), dma((2,)),
            dma((1,)), dma((10,)), dma((1,)), dma((6,)),
            dma((4,)), dma((2,)), dma((3,)), dma((1,)), dma((2, 4, 2)), dma((3,)),
        ],
        compiler_params=pltpu.CompilerParams(collective_id=0, has_side_effects=True),
    )(*operands)
    return out.swapaxes(2, 3)


def solution(mesh):
    in_specs = (
        P("replica", "tm", None, None, None),
        P(None, None, "fsdp"),
        P(None, "fsdp", None),
        P("replica", "tm", None, None, None),
        P(),
        P(None, "fsdp", None),
        P(None, "fsdp", ("replica", "tm")),
    )
    out_specs = P(None, None, "fsdp", ("replica", "tm"))
    return jax.shard_map(shards, mesh=mesh, in_specs=in_specs, out_specs=out_specs, check_vma=False)
```
